256 devices in a mesh: seq: 64 (over z, x, core), head: 4 (over y).
Axes of the slice: x: 4, y: 4, z: 8, core: 2. Of those that a mesh axis runs over, the one named last changes fastest.
Arguments:
- queries: float32 [16384, 4096], P('seq', 'head'), may hold values from -0.54 to 0.54
- key_input: float32 [16384, 4096], P('seq', 'head'), may hold values from -0.54 to 0.54
- value_input: float32 [16384, 4096], P('seq', 'head'), may hold values from -6 to 6
- grad_output: float32 [16384, 4096], P('seq', 'head'), may hold values from -0.54 to 0.54
- log_decay: float32 [16384, 32], P('seq', 'head'), may hold values from -2 to 0
- level_weight: float32 [16384, 7], P('seq'), may hold values from 0.3 to 1.5
- segment: int32 [16384], P('seq'), may hold values from 0 to 3, never falling along the last dimension, each value on 1 to 8192 neighbouring positions
Outputs:
- grad_query: float32 [16384, 4096], P('seq', 'head')
- grad_key: float32 [16384, 4096], P('seq', 'head')
- grad_value: float32 [16384, 4096], P('seq', 'head')
- grad_level: float32 [16384, 7], P('seq')
The draws below stay inside these ranges and needn't reach their ends.
Inputs may be any that keep to these rules, and one draw needn't show every extreme that they name: `segment`: document numbers never fall along the tokens; each document has at most 8192 tokens, one exactly that many.
All inputs are finite; a program needn't handle non-finite values.
Results may differ from the reference program's by a relative error of at most 0.00012.
Values sent between devices are 32-bit elements; how exact they have to be, the bound alone decides.
A program may use at most 128 MiB of HBM per device.

```python
import math
import jax
import jax.numpy as jnp
import numpy as np
from jax import lax

HEAD_TOTAL = 32
HEAD_DIM = 128
STRETCH = 256
LEVELS = 7
NDOC = 4
D = 4096
TOKEN_TOTAL = 16384
NB = 6


def draw_log_decay(key, part):
    fragment_list = jax.random.split(key, 7)
    fast_share = 0.5
    fast_heads = jax.random.uniform(fragment_list[0], (HEAD_TOTAL,)) < fast_share
    fast_rate = jnp.exp(jax.random.uniform(fragment_list[1], (HEAD_TOTAL,), minval=jnp.log(0.02), maxval=jnp.log(0.04)))
    slow_rate = jnp.exp(jax.random.uniform(fragment_list[2], (HEAD_TOTAL,), minval=jnp.log(0.02), maxval=jnp.log(0.2))) / TOKEN_TOTAL
    decay_rate = jnp.where(fast_heads, fast_rate, slow_rate)
    block_factor = jax.random.uniform(fragment_list[3], (TOKEN_TOTAL // STRETCH, HEAD_TOTAL), minval=0.5, maxval=2.0)
    token_factor = jax.random.uniform(fragment_list[4], (TOKEN_TOTAL, HEAD_TOTAL), minval=0.5, maxval=2.0)
    stable_mode = -decay_rate[None, :] * jnp.repeat(block_factor, STRETCH, axis=0) * token_factor
    flush_location = jax.random.randint(fragment_list[5], (2, HEAD_TOTAL), 0, TOKEN_TOTAL)
    flush_depth = jax.random.uniform(fragment_list[6], (2, HEAD_TOTAL), minval=0.22, maxval=0.69)
    token_offsets = jnp.arange(TOKEN_TOTAL, dtype=jnp.int32)[:, None, None]
    flush_events = jnp.sum(jnp.where(token_offsets == flush_location[None], flush_depth[None], 0.0), axis=1)
    return (stable_mode - flush_events).astype(jnp.float32)


def steps_of(rng, dims, pieces, low, high):
    def one(dim, blocks):
        steps = jax.random.uniform(jax.random.fold_in(jax.random.fold_in(rng, 6), dim), (blocks,), jnp.float32, low / len(pieces), high / len(pieces))
        return jnp.repeat(jnp.exp(steps), dims[dim] // blocks).reshape((-1,) + (1,) * (len(dims) - dim - 1))

    factor_of = one(*pieces[0])
    for cut in pieces[1:]:
        factor_of = factor_of * one(*cut)
    return factor_of


def profile(count, total, reach, lean):
    portions = [(1 << 20) // math.isqrt(grade ** lean) + 1 for grade in range(2, count + 1)]
    surplus, holding = total - reach - (count - 1), [1] * (count - 1)
    while surplus > 0:
        candidates = [i for i in range(count - 1) if holding[i] < reach]
        pool, left = sum([portions[i] for i in candidates]), surplus
        for i in candidates:
            addition = min(reach - holding[i], max(1, left * portions[i] // pool), surplus)
            holding[i] = holding[i] + addition
            surplus = surplus - addition
    return np.array([reach] + holding)


def uneven_parts(own_key, count, total, bound, skew):
    if count == 2:
        one = jax.random.randint(own_key, (), max(1, total - bound), min(bound, total - 1) + 1)
        return jnp.stack([one, total - one])
    tallies = jnp.asarray(profile(count, total, bound, skew), jnp.int32)
    twos = (count - 1) // 2
    source_of, receiver = tallies[1:1 + 2 * twos:2], tallies[2:2 + 2 * twos:2]
    margin = jnp.minimum(source_of - 1, bound - receiver)
    moved = jax.random.randint(jax.random.fold_in(own_key, 1), (twos,), 0, 1 << 20) % (margin + 1)
    tallies = tallies.at[1:1 + 2 * twos:2].set(source_of - moved).at[2:2 + 2 * twos:2].set(receiver + moved)
    return tallies[jax.random.permutation(jax.random.fold_in(own_key, 2), count)]


def noise(stream_key, shape, deviation, reach, pieces=(), kind=jnp.bfloat16):
    loudness = steps_of(stream_key, shape, pieces, -0.22, 0.18) if pieces else 1.0
    array = jax.random.normal(stream_key, shape, jnp.float32) * deviation * loudness
    return jnp.minimum(jnp.maximum(array, -reach), reach).astype(kind)


def setup_inputs(seed: int = 0) -> dict:
    key_list = jax.random.split(jax.random.key(seed), 8)
    queries = noise(key_list[0], (TOKEN_TOTAL, D), 0.09, 0.54, ((0, 64), (1, 4)), jnp.float32)
    key_input = noise(key_list[1], (TOKEN_TOTAL, D), 0.09, 0.54, ((0, 64), (1, 4)), jnp.float32)
    value_input = noise(key_list[2], (TOKEN_TOTAL, D), 1.0, 6.0, ((0, 64), (1, 4)), jnp.float32)
    grad_output = noise(key_list[3], (TOKEN_TOTAL, D), 0.09, 0.54, ((0, 64), (1, 4)), jnp.float32)
    log_decay = draw_log_decay(jax.random.fold_in(key_list[7], 71), 0)
    level_weight = jnp.clip(jnp.exp(math.log(1.5) - 1.60943787 * jax.random.uniform(key_list[5], (TOKEN_TOTAL, LEVELS), jnp.float32) ** steps_of(key_list[5], (TOKEN_TOTAL, LEVELS), ((0, 64),), -0.2, 0.2)), 0.3, 1.5)
    segment = jnp.searchsorted(jnp.cumsum(uneven_parts(key_list[6], NDOC, TOKEN_TOTAL, TOKEN_TOTAL // 2, 0)), jnp.arange(TOKEN_TOTAL), side="right").astype(jnp.int32)
    return {"queries": queries, "key_input": key_input, "value_input": value_input, "grad_output": grad_output, "log_decay": log_decay, "level_weight": level_weight, "segment": segment}


PRECISE = lax.Precision.HIGHEST


def stretch_spans(totals):
    stretches = totals.shape[0]
    stretch_ids = jnp.arange(stretches, dtype=jnp.int32)
    inside = (stretch_ids[None, None, :] > stretch_ids[:, None, None]) & (stretch_ids[None, None, :] <= stretch_ids[None, :, None])
    return jnp.sum(jnp.where(inside, totals[None, None, :], 0.0), axis=2)


def head_grads(queries, key_input, value_input, grad_output, log_decay, level_weight, segment):
    stretches = queries.shape[0]
    cumulative = jnp.cumsum(log_decay, axis=1)
    totals = cumulative[:, -1]
    stretch_ends = segment[:, -1]
    spans = stretch_spans(totals)
    position = jnp.arange(STRETCH, dtype=jnp.int32)
    visible = (position[None, :, None] >= position[None, None, :]) & (segment[:, :, None] == segment[:, None, :])
    decay_gap = cumulative[:, :, None] - cumulative[:, None, :]
    within = jnp.where(visible, jnp.exp(jnp.minimum(decay_gap, 0.0)), 0.0)
    scores = jnp.einsum('ctd,csd->cts', queries, key_input, precision=PRECISE)
    grad_scores = jnp.einsum('ctd,csd->cts', grad_output, value_input, precision=PRECISE)
    weight = within * level_weight[:, :, 0][:, :, None]
    head_value = jnp.einsum('cts,ctd->csd', weight * scores, grad_output, precision=PRECISE)
    head_query = jnp.einsum('cts,csd->ctd', weight * grad_scores, key_input, precision=PRECISE)
    head_key = jnp.einsum('cts,ctd->csd', weight * grad_scores, queries, precision=PRECISE)
    level_grads = [jnp.sum(within * scores * grad_scores, axis=2)]
    source_weight = jnp.exp(totals[:, None] - cumulative) * (segment == stretch_ends[:, None]).astype(jnp.float32)
    states = jnp.einsum('csi,csj->cij', source_weight[:, :, None] * key_input, value_input, precision=PRECISE)
    stretch_ids = jnp.arange(stretches, dtype=jnp.int32)
    grad_states = jnp.zeros_like(states)
    for level in range(1, NB + 1):
        half_size = 1 << (level - 1)
        upper_half = ((stretch_ids >> (level - 1)) & 1) == 1
        lower_end = ((stretch_ids >> level) << level) + half_size - 1
        member = upper_half[:, None] & (stretch_ids[None, :] >= lower_end[:, None] - half_size + 1) & (stretch_ids[None, :] <= lower_end[:, None])
        source_span = spans[:, lower_end].T
        linked = member & (stretch_ends[None, :] == stretch_ends[lower_end][:, None])
        carried = jnp.where(linked, jnp.exp(jnp.where(linked, source_span, 0.0)), 0.0)
        blocks = jnp.einsum('cx,xij->cij', carried, states, precision=PRECISE)
        before = jnp.maximum(stretch_ids - 1, 0)
        query_span = spans[lower_end, before]
        factor = jnp.where(upper_half[:, None] & (segment == stretch_ends[lower_end][:, None]), jnp.exp(cumulative + query_span[:, None]), 0.0)
        level_scale = factor * level_weight[:, :, level]
        head_query = head_query + level_scale[:, :, None] * jnp.einsum('ctj,cij->cti', grad_output, blocks, precision=PRECISE)
        reached = jnp.einsum('cti,cij->ctj', queries, blocks, precision=PRECISE)
        level_grads.append(factor * jnp.sum(reached * grad_output, axis=2))
        grad_blocks = jnp.einsum('cti,ctj->cij', level_scale[:, :, None] * queries, grad_output, precision=PRECISE)
        grad_states = grad_states + jnp.einsum('cx,cij->xij', carried, grad_blocks, precision=PRECISE)
    head_key = head_key + source_weight[:, :, None] * jnp.einsum('csj,cij->csi', value_input, grad_states, precision=PRECISE)
    head_value = head_value + source_weight[:, :, None] * jnp.einsum('csi,cij->csj', key_input, grad_states, precision=PRECISE)
    for level in range(NB + 1, LEVELS):
        level_grads.append(jnp.zeros_like(level_grads[0]))
    return head_query, head_key, head_value, jnp.stack(level_grads, axis=2)


def reference(queries, key_input, value_input, grad_output, log_decay, level_weight, segment):
    stretches = TOKEN_TOTAL // STRETCH

    def split_heads(tensor):
        return tensor.reshape(stretches, STRETCH, HEAD_TOTAL, HEAD_DIM).transpose(2, 0, 1, 3)

    def merge_heads(tensor):
        return tensor.transpose(1, 2, 0, 3).reshape(TOKEN_TOTAL, HEAD_TOTAL * HEAD_DIM)

    decay_heads = log_decay.reshape(stretches, STRETCH, HEAD_TOTAL).transpose(2, 0, 1)
    weight_rows = level_weight.reshape(stretches, STRETCH, LEVELS)
    segment_rows = segment.reshape(stretches, STRETCH)

    def one_head(head_items):
        return head_grads(head_items[0], head_items[1], head_items[2], head_items[3], head_items[4], weight_rows, segment_rows)

    head_query, head_key, head_value, head_level = lax.map(one_head, (split_heads(queries), split_heads(key_input), split_heads(value_input), split_heads(grad_output), decay_heads))
    grad_level = jnp.sum(head_level, axis=0).reshape(TOKEN_TOTAL, LEVELS)
    return merge_heads(head_query), merge_heads(head_key), merge_heads(head_value), grad_level
```

```python
import jax
import jax.numpy as jnp
from jax import lax
from jax.experimental import pallas as pl
from jax.experimental.pallas import tpu as pltpu
from jax.sharding import PartitionSpec as P

F32 = jnp.float32
BF16 = jnp.bfloat16
NZ, NX = 8, 4
LV_ALL = 7
LV = 6


def split(a):
    hi = a.astype(BF16)
    return hi, (a - hi.astype(F32)).astype(BF16)


def left(a, axis):
    hi, lo = split(a)
    return jnp.concatenate([hi, hi, lo], axis=axis)


def right(a, axis):
    hi, lo = split(a)
    return jnp.concatenate([hi, lo, hi], axis=axis)


def mm(a, b, ca, cb):
    return lax.dot_general(a, b, (((ca,), (cb,)), ((), ())), preferred_element_type=F32)


def loop(n, fn):
    def body(i, carry):
        fn(i)
        return carry

    lax.fori_loop(0, n, body, 0)


def kernel(pack, q, k, v, o, dq, dk, dv, gl,
           cumcol, ecol, swcol, lwcol, cumt, bias, bfac, gfac, lev,
           pb, zt, st, rf, tt, gs, gr, mz, rz, lam, mx, rx, rl, ml, hb,
           s_g, r_g, s_1, r_1, s_x, r_x, s_z, r_z, s_f, r_f, s_p, r_p,
           s_bz, r_bz, s_bx, r_bx, s_b1, r_b1, s_h, r_h):
    n, heads, w = pack.shape[0], swcol.shape[0], 128
    half = heads // 2
    me = lax.axis_index("seq")
    hd = lax.axis_index("head")
    nh = 4
    core = me % 2
    x = (me // 2) % NX
    z = me // (2 * NX)
    bits = [core, x % 2, x // 2, z % 2, (z // 2) % 2, z // 4]

    def at(zz, xx, cc):
        return ((zz * NX + xx) * 2 + cc, hd)

    partner = at(z, x, 1 - core)

    def cp(src, dst, ss, rs, dev):
        return pltpu.make_async_remote_copy(
            src_ref=src, dst_ref=dst, send_sem=ss, recv_sem=rs,
            device_id=dev, device_id_type=pl.DeviceIdType.MESH)

    barrier = pltpu.get_barrier_semaphore()
    peers = [partner]
    peers += [at(z, (x + d) % NX, core) for d in range(1, NX)]
    peers += [at((z + d) % NZ, x, core) for d in range(1, NZ)]
    peers += [(me, (hd + d) % nh) for d in range(1, nh)]
    for dev in peers:
        pl.semaphore_signal(barrier, inc=1, device_id=dev, device_id_type=pl.DeviceIdType.MESH)

    pk = pack[...]
    rows = lax.broadcasted_iota(jnp.int32, (n, n), 0)
    cols = lax.broadcasted_iota(jnp.int32, (n, n), 1)
    tri = (cols <= rows).astype(BF16)
    p1 = pk.astype(BF16)
    rest = pk - p1.astype(F32)
    p2 = rest.astype(BF16)
    p3 = (rest - p2.astype(F32)).astype(BF16)
    cum = mm(tri, p1, 1, 0) + mm(tri, p2, 1, 0) + mm(tri, p3, 1, 0)
    total = cum[n - 1:n, :]
    seg = pk[:, 15:16]
    own_end = pk[n - 1:n, 15:16]
    lane1 = lax.broadcasted_iota(jnp.int32, (1, w), 1)
    own_row = jnp.where(lane1 == heads, jnp.broadcast_to(own_end, (1, w)), total)
    r0 = x * 2 + core
    pb[r0] = jnp.broadcast_to(own_row, (8, w))

    pl.semaphore_wait(barrier, len(peers))

    def g1():
        return cp(pb.at[r0], pb.at[r0], s_g.at[0], r_g.at[0], partner)

    def g2(d):
        slot = pb.at[pl.ds(2 * x, 2)]
        return cp(slot, slot, s_g.at[d], r_g.at[d], at(z, (x + d) % NX, core))

    def g3(d):
        return cp(zt.at[z], zt.at[z], s_g.at[3 + d], r_g.at[3 + d], at((z + d) % NZ, x, core))

    g1().start()
    sw = jnp.exp(total - cum) * (seg == own_end).astype(F32)
    for h in range(heads):
        swcol[h] = jnp.broadcast_to(sw[:, h:h + 1], (n, w))

    def f1_send(h):
        return cp(st.at[h], rf.at[0, h], s_1.at[h], r_1.at[h], partner)

    def head_cols(h):
        return pl.ds(pl.multiple_of(h * w, w), w)

    def make_state(h):
        vt = v[:, head_cols(h)].T
        st[h] = mm(left(vt, 1), right(k[:, head_cols(h)] * swcol[h], 0), 1, 0)

        @pl.when(h < half + half * (1 - core))
        def _():
            f1_send(h).start()

    def first_half(i):
        make_state(i)

    loop(half, first_half)
    g1().wait_recv()
    for d in range(1, NX):
        g2(d).start()
    loop(half, lambda i: make_state(half + i))
    for d in range(1, NX):
        g2(d).wait_recv()
    sub = lax.broadcasted_iota(jnp.int32, (8, w), 0)
    lane8 = lax.broadcasted_iota(jnp.int32, (8, w), 1)
    plane = jnp.zeros((8, w), F32)
    for r in range(8):
        plane = jnp.where(sub == r, pb[r], plane)
    zt[z] = plane
    for d in range(1, NZ):
        g3(d).start()
    for h in range(heads):
        cumcol[h] = jnp.broadcast_to(cum[:, h:h + 1], (n, w))
    for l in range(LV_ALL):
        lwcol[l] = jnp.broadcast_to(pk[:, 8 + l:9 + l], (n, w))
    cumt[...] = cum.T
    pkt = pk.T
    segrow = pkt[15:16, :]
    vis = (cols <= rows) & (jnp.broadcast_to(seg, (n, n)) == jnp.broadcast_to(segrow, (n, n)))
    bias[...] = jnp.where(vis, 0.0, -1e30)
    for l in range(LV_ALL):
        lev[l] = jnp.zeros((n, w), F32)
    for d in range(1, NZ):
        g3(d).wait_recv()
    tbl = zt[...].reshape(8 * NZ, w)
    idx = lax.broadcasted_iota(jnp.int32, (8 * NZ, w), 0)

    def row(c):
        return jnp.sum(jnp.where(idx == c, tbl, 0.0), axis=0, keepdims=True)

    def span(lo, hi):
        return jnp.sum(jnp.where((idx > lo) & (idx <= hi), tbl, 0.0), axis=0, keepdims=True)

    def same(a, b):
        return (row(a)[:, heads:heads + 1] == row(b)[:, heads:heads + 1]).astype(F32)

    def spread(vec):
        m = jnp.where(lane8 == sub, jnp.broadcast_to(vec, (8, w)), 0.0)
        return jnp.broadcast_to(jnp.sum(m, axis=1, keepdims=True), (8, w))

    for l in range(LV):
        hs = 1 << l
        low = (me // (2 * hs)) * (2 * hs) + hs - 1
        up = low + hs
        u = bits[l].astype(F32)
        g = jnp.exp(jnp.minimum(span(low, me - 1), 0.0)) * same(low, me - 1) * u
        b = jnp.exp(jnp.minimum(span(low, up), 0.0)) * same(low, up)
        gfac[l] = spread(g)
        bfac[l] = spread(b)
    prev_end = row(me - 1)[:, heads:heads + 1]
    ecum = jnp.exp(cum) * (seg == prev_end).astype(F32)
    for h in range(heads):
        ecol[h] = jnp.broadcast_to(ecum[:, h:h + 1], (n, w))

    def bf(l, h):
        return bfac[l, pl.ds(h, 1), :]

    def gf(l, h):
        return gfac[l, pl.ds(h, 1), :]

    def own(i):
        return core * half + i

    def mix(l, h, mine, theirs):
        b = bf(l, h)
        u = bits[l] == 1
        ca = jnp.where(u, 1.0, b)
        cb = jnp.where(u, b, 1.0)
        return ca * mine + cb * theirs

    def fx_send(j, i):
        to = at(z, x + 1 - 2 * (x % 2), core) if j == 0 else at(z, NX - 1 - x, core)
        return cp(tt.at[j, i], rf.at[1 + j, own(i)], s_x.at[j, i], r_x.at[j, i], to)

    def fwd(l, i):
        slot = rf.at[l, own(i)]
        return cp(slot, slot, s_f.at[l - 1, i], r_f.at[l - 1, i], partner)

    def fwd_in(l, i):
        slot = rf.at[l, half * (1 - core) + i]
        return cp(slot, slot, s_f.at[l - 1, i], r_f.at[l - 1, i], partner)

    def f1(i):
        h = own(i)
        f1_send(h).wait_recv()
        tt[0, i] = mix(0, h, st[h], rf[0, h])
        fx_send(0, i).start()

    def fx(j):
        def one(i):
            h = own(i)
            fx_send(j, i).wait_recv()

            @pl.when(bits[1 + j] == 1)
            def _():
                fwd(1 + j, i).start()

            tt[1 + j, i] = mix(1 + j, h, tt[j, i], rf[1 + j, h])
            if j == 0:
                fx_send(1, i).start()
            else:
                @pl.when(z % 2 == 0)
                def _():
                    fz_send(0, tt.at[2, i], i).start()

        return one

    def fz_send(m, src, i):
        return cp(src, rf.at[3 + m, own(i)], s_z.at[m, i], r_z.at[m, i], at((z + 1) % NZ, x, core))

    def fz_wait(m, i):
        fz_send(m, rf.at[3 + m, own(i)], i).wait_recv()

    def f4(i):
        h = own(i)
        fz_wait(0, i)
        fwd(3, i).start()
        tt[3, i] = bf(3, h) * rf[3, h] + tt[2, i]

        @pl.when((z // 2) % 2 == 0)
        def _():
            fz_send(1, tt.at[3, i], i).start()

    def f5(i):
        h = own(i)
        fz_wait(1, i)

        @pl.when(z % 2 == 0)
        def _():
            fz_send(1, rf.at[4, h], i).start()

        @pl.when(z == 3)
        def _():
            tt[4, i] = bf(4, h) * rf[4, h] + tt[3, i]
            fz_send(2, tt.at[4, i], i).start()

        fwd(4, i).start()

    def f6(i):
        fz_wait(2, i)

        @pl.when(z < NZ - 1)
        def _():
            fz_send(2, rf.at[5, own(i)], i).start()

        fwd(5, i).start()

    def gp_send(l, i):
        return cp(gs.at[l, half * (1 - core) + i], gr.at[l - 1, i], s_p.at[l - 1, i], r_p.at[l - 1, i], partner)

    def make_g(h):
        lhs = left(o[:, head_cols(h)].T, 1)
        qe = q[:, head_cols(h)] * ecol[h]
        for l in range(0, LV, 2):
            a = jnp.concatenate([qe * lwcol[l + 1], qe * lwcol[l + 2]], axis=1)
            both = mm(lhs, right(a, 0), 1, 0)
            gs[l, h] = both[:, :w] * gf(l, h)
            gs[l + 1, h] = both[:, w:] * gf(l + 1, h)

    def g_other(i):
        make_g(half * (1 - core) + i)
        for l in range(1, LV):
            @pl.when(bits[l] == 1)
            def _():
                gp_send(l, i).start()

    def b1_early(i):
        return cp(gs.at[0, i], rl.at[i], s_b1.at[i], r_b1.at[i], partner)

    def g_own(i):
        make_g(own(i))

    def bz_send(m, i):
        return cp(mz.at[m, i], rz.at[m, i], s_bz.at[m, i], r_bz.at[m, i], at((z + NZ - 1) % NZ, x, core))

    def gsum(l, i):
        return gs[l, own(i)] + gr[l - 1, i]

    def gp_wait(l, i):
        gp_send(l, i).wait_recv()

    def bwave(zc):
        b0, b1, b2 = zc & 1, zc >> 1 & 1, zc >> 2 & 1
        slots = [m for m in range(3) if (zc + 1) < NZ and ((zc + 1) >> m & 1) and (m > 0 or not b0)]

        def one(i):
            h = own(i)
            for m in range(3):
                if zc >> m & 1:
                    gp_wait(3 + m, i)
            got = {}
            for m in reversed(slots):
                bz_send(m, i).wait_recv()
                got[m] = rz[m, i]
            if not b0:
                down = got[0]
            elif zc in (1, 5):
                down = got[1]
            elif zc == 3:
                down = got[2]
            else:
                down = None
            if b2:
                mz[2, i] = gsum(5, i) + got[2] if 2 in got else gsum(5, i)
                bz_send(2, i).start()
            if b1:
                if zc == 3:
                    mz[1, i] = gsum(4, i) + bf(4, h) * down
                elif zc == 7:
                    mz[1, i] = gsum(4, i)
                else:
                    mz[1, i] = gsum(4, i) + got[1]
                bz_send(1, i).start()
            if b0:
                mz[0, i] = gsum(3, i) if down is None else gsum(3, i) + bf(3, h) * down
                bz_send(0, i).start()
            lam[0, i] = jnp.zeros((w, w), F32) if down is None else down

        return one

    def bx_send(j, i):
        to = at(z, NX - 1 - x, core) if j == 0 else at(z, x + 1 - 2 * (x % 2), core)
        return cp(mx.at[j, i], rx.at[j, i], s_bx.at[j, i], r_bx.at[j, i], to)

    def bx_out(j):
        l = 2 - j

        def one(i):
            h = own(i)

            @pl.when(bits[l] == 1)
            def _():
                gp_wait(l, i)
                mx[j, i] = gsum(l, i) + bf(l, h) * lam[j, i]

            @pl.when(bits[l] == 0)
            def _():
                mx[j, i] = lam[j, i]

            bx_send(j, i).start()

        return one

    def bx_in(j):
        l = 2 - j

        def one(i):
            bx_send(j, i).wait_recv()
            keep = jnp.where(bits[l] == 1, 1.0, bf(l, own(i)))
            lam[j + 1, i] = keep * lam[j, i] + rx[j, i]

        return one

    def b1_up(i):
        return cp(ml.at[i], rl.at[own(i)], s_b1.at[half + i], r_b1.at[half + i], partner)

    def b1_up_in(i):
        return cp(ml.at[i], rl.at[half * (1 - core) + i], s_b1.at[half + i], r_b1.at[half + i], partner)

    def b1(i):
        h = own(i)

        @pl.when(core == 1)
        def _():
            ml[i] = bf(0, h) * lam[2, i] + gs[0, h]
            rl[h] = lam[2, i]

        @pl.when(core == 0)
        def _():
            ml[i] = lam[2, i]
            b1_early(i).wait_recv()
            rl[h] = bf(0, h) * lam[2, i] + rl[h]

        b1_up(i).start()

    def inside(h):
        hc = head_cols(h)
        qh, kh, vh, oh = q[:, hc], k[:, hc], v[:, hc], o[:, hc]
        cc = cumcol[h]
        gap = jnp.concatenate([cc, cc], axis=1) - cumt[pl.ds(h, 1), :]
        within = jnp.exp(jnp.minimum(gap, 0.0) + bias[...])
        sc = mm(left(qh, 1), right(kh, 1), 1, 1)
        go = mm(left(oh, 1), right(vh, 1), 1, 1)
        lw = lwcol[0]
        wt = within * jnp.concatenate([lw, lw], axis=1)
        prod = within * sc * go
        lev[0] += prod[:, :w] + prod[:, w:]
        a = wt * sc
        b = wt * go
        dq[:, hc] = mm(left(b, 1), right(kh, 0), 1, 0)
        dv[:, hc] = mm(left(a.T, 1), right(oh, 0), 1, 0)
        dk[:, hc] = mm(left(b.T, 1), right(qh, 0), 1, 0)

    def levels(h):
        hc = head_cols(h)
        oh = left(o[:, hc], 1)
        qh = q[:, hc]
        e = ecol[h]
        acc = dq[:, hc]
        for l in range(0, LV, 2):
            pair = []
            for m in (l, l + 1):
                pair.append(jnp.where(bits[m] == 1, rf[m, h] * gf(m, h), 0.0))
            back = mm(oh, right(jnp.concatenate(pair, axis=1), 0), 1, 0)
            for m in (l, l + 1):
                part = e * back[:, (m - l) * w:(m - l + 1) * w]
                lev[m + 1] += qh * part
                acc = acc + lwcol[m + 1] * part
        dq[:, hc] = acc

    def sources(h):
        hc = head_cols(h)
        g = rl[h]
        s = swcol[h]
        dk[:, hc] += s * mm(left(v[:, hc], 1), right(g, 0), 1, 0)
        dv[:, hc] += s * mm(left(k[:, hc], 1), right(g, 1), 1, 1)

    loop(half, f1)
    loop(half, g_other)
    loop(half, fx(0))
    loop(half, g_own)

    @pl.when(core == 1)
    def _():
        loop(half, lambda i: b1_early(i).start())

    loop(half, fx(1))
    for zc in range(NZ - 1, 3, -1):
        @pl.when(z == zc)
        def _():
            loop(half, bwave(zc))

    @pl.when(z % 2 == 1)
    def _():
        loop(half, f4)

    @pl.when((z // 2) % 2 == 1)
    def _():
        loop(half, f5)

    @pl.when(z == 4)
    def _():
        loop(half, f6)

    loop(heads, inside)
    for zc in range(3, -1, -1):
        @pl.when(z == zc)
        def _():
            loop(half, bwave(zc))

    loop(half, bx_out(0))
    loop(half, bx_in(0))
    loop(half, bx_out(1))
    loop(half, bx_in(1))
    loop(half, b1)

    @pl.when(z > 4)
    def _():
        loop(half, f6)

    @pl.when(core == 1)
    def _():
        loop(half, lambda i: f1_send(i).wait_recv())

    for l in range(1, LV):
        @pl.when(bits[l] == 1)
        def _():
            loop(half, lambda i: fwd_in(l, i).wait_recv())

    loop(heads, levels)
    loop(half, lambda i: b1_up_in(i).wait_recv())
    loop(heads, sources)

    lanes = lax.broadcasted_iota(jnp.int32, (n, w), 1)
    acc = jnp.zeros((n, w), F32)
    for l in range(LV_ALL):
        acc = jnp.where(lanes == l, jnp.sum(lev[l], axis=1, keepdims=True), acc)
    hb[hd] = acc.T[:8, :]

    def h_send(d):
        return cp(hb.at[hd], hb.at[hd], s_h.at[d - 1], r_h.at[d - 1], (me, (hd + d) % nh))

    for d in range(1, nh):
        h_send(d).start()
    for d in range(1, nh):
        h_send(d).wait_recv()
    tot = hb[0] + hb[1] + hb[2] + hb[3]
    full = jnp.concatenate([tot, jnp.zeros((w - 8, n), F32)], axis=0).T
    gl[...] = full[:, :LV_ALL]

    for d in range(1, nh):
        h_send(d).wait_send()
    g1().wait_send()
    for d in range(1, NX):
        g2(d).wait_send()
    for d in range(1, NZ):
        g3(d).wait_send()
    loop(half, lambda i: f1_send(i).wait_send())

    @pl.when(core == 0)
    def _():
        loop(half, lambda i: f1_send(half + i).wait_send())

    @pl.when(core == 1)
    def _():
        loop(half, lambda i: b1_early(i).wait_send())

    for j in range(2):
        loop(half, lambda i: fx_send(j, i).wait_send())
        loop(half, lambda i: bx_send(j, i).wait_send())
    loop(half, lambda i: b1_up(i).wait_send())
    for l in range(1, LV):
        @pl.when(bits[l] == 1)
        def _():
            loop(half, lambda i: fwd(l, i).wait_send())
            loop(half, lambda i: gp_send(l, i).wait_send())

    up = [z % 2 == 0,
          (z % 4 == 1) | (z % 4 == 2),
          (z >= 3) & (z <= 6)]
    for m in range(3):
        @pl.when(up[m])
        def _():
            loop(half, lambda i: fz_send(m, tt.at[2, i], i).wait_send())

        @pl.when(bits[3 + m] == 1)
        def _():
            loop(half, lambda i: bz_send(m, i).wait_send())


def on_device(queries, key_input, value_input, grad_output, log_decay, level_weight, segment):
    n, heads = log_decay.shape
    width = queries.shape[1]
    w = 128
    half = heads // 2
    pack = jnp.concatenate(
        [log_decay, level_weight, segment.astype(F32)[:, None],
         jnp.zeros((n, w - heads - LV_ALL - 1), F32)], axis=1)
    dma = pltpu.SemaphoreType.DMA
    vmem = pltpu.VMEM
    scratch = [
        vmem((heads, n, w), F32),
        vmem((heads, n, w), F32),
        vmem((heads, n, w), F32),
        vmem((LV_ALL, n, w), F32),
        vmem((w, n), F32),
        vmem((n, n), F32),
        vmem((LV, 8, w), F32),
        vmem((LV, 8, w), F32),
        vmem((LV_ALL, n, w), F32),
        vmem((8, 8, w), F32),
        vmem((NZ, 8, w), F32),
        vmem((heads, w, w), F32),
        vmem((LV, heads, w, w), F32),
        vmem((5, half, w, w), F32),
        vmem((LV, heads, w, w), F32),
        vmem((LV - 1, half, w, w), F32),
        vmem((3, half, w, w), F32),
        vmem((3, half, w, w), F32),
        vmem((3, half, w, w), F32),
        vmem((2, half, w, w), F32),
        vmem((2, half, w, w), F32),
        vmem((heads, w, w), F32),
        vmem((half, w, w), F32),
        vmem((4, 8, n), F32),
    ]
    for shape in ((11,), (heads,), (2, half), (3, half), (LV - 1, half), (LV - 1, half),
                  (3, half), (2, half), (heads,), (3,)):
        scratch += [dma(shape), dma(shape)]
    spec = pl.BlockSpec(memory_space=pltpu.VMEM)
    out = jax.ShapeDtypeStruct((n, width), F32)
    return pl.pallas_call(
        kernel,
        out_shape=(out, out, out, jax.ShapeDtypeStruct((n, LV_ALL), F32)),
        in_specs=[spec] * 5,
        out_specs=(spec,) * 4,
        scratch_shapes=scratch,
        compiler_params=pltpu.CompilerParams(
            collective_id=0, has_side_effects=True, vmem_limit_bytes=60 << 20),
    )(pack, queries, key_input, value_input, grad_output)


def solution(mesh):
    in_specs = (
        P("seq", "head"),
        P("seq", "head"),
        P("seq", "head"),
        P("seq", "head"),
        P("seq", "head"),
        P("seq", None),
        P("seq"),
    )
    out_specs = (P("seq", "head"), P("seq", "head"), P("seq", "head"), P("seq", None))
    return jax.shard_map(
        on_device, mesh=mesh, in_specs=in_specs, out_specs=out_specs, check_vma=False
    )
```

```python
import jax
import jax.numpy as jnp
from jax import lax
from jax.experimental import pallas as pl
from jax.experimental.pallas import tpu as pltpu
from jax.sharding import PartitionSpec as P

F32 = jnp.float32
BF16 = jnp.bfloat16
NZ, NX = 8, 4
LV_ALL = 7
LV = 6


def split(a):
    hi = a.astype(BF16)
    return hi, (a - hi.astype(F32)).astype(BF16)


def left(a, axis):
    hi, lo = split(a)
    return jnp.concatenate([hi, hi, lo], axis=axis)


def right(a, axis):
    hi, lo = split(a)
    return jnp.concatenate([hi, lo, hi], axis=axis)


def mm(a, b, ca, cb):
    return lax.dot_general(a, b, (((ca,), (cb,)), ((), ())), preferred_element_type=F32)


def loop(n, fn):
    def body(i, carry):
        fn(i)
        return carry

    lax.fori_loop(0, n, body, 0)


def kernel(ldt, lwt, sgt, q_hbm, k_hbm, v_hbm, o_hbm, dq_hbm, dk_hbm, dv_hbm, glt,
           q, k, v, o, dq, dk, dv, packt,
           cumcol, ecol, swcol, lwcol, cumt, bias, bfac, gfac, pfac, lev,
           pb, zt, st, rf, tt, t01, rsb, zs, gs, gr, gx, rsg, gp, za, rz6, rz5, rz4, db,
           m3, r3, m2, r2, rl, ml, hb,
           s_in, s_out, s_g, r_g, s_1, r_1, s_rs, r_rs, s_x, r_x, s_z, r_z, s_ag, r_ag, s_f, r_f, s_p, r_p,
           s_bs, r_bs, s_bz, r_bz, s_d, r_d, s_m, r_m, s_b1, r_b1, s_h, r_h):
    n, heads, w = q.shape[0], swcol.shape[0], 128
    half = heads // 2
    me = lax.axis_index("seq")
    hd = lax.axis_index("head")
    nh = 4
    core = me % 2
    x = (me // 2) % NX
    z = me // (2 * NX)
    bits = [core, x % 2, x // 2, z % 2, (z // 2) % 2, z // 4]
    r0 = x * 2 + core

    def at(zz, xx, cc):
        return ((zz * NX + xx) * 2 + cc, hd)

    partner = at(z, x, 1 - core)

    def cp(src, dst, ss, rs, dev):
        return pltpu.make_async_remote_copy(
            src_ref=src, dst_ref=dst, send_sem=ss, recv_sem=rs,
            device_id=dev, device_id_type=pl.DeviceIdType.MESH)

    def bring(j):
        src, dst = ((k_hbm, k), (v_hbm, v), (o_hbm, o), (q_hbm, q))[j]
        return pltpu.make_async_copy(src, dst, s_in.at[j])

    for j in range(4):
        bring(j).start()

    barrier = pltpu.get_barrier_semaphore()
    plane_peers = [(d, e) for d in range(NX) for e in range(2) if (d, e) != (0, 0)]

    def plane_dev(d, e):
        return at(z, (x + d) % NX, (core + e) % 2)

    peers = [plane_dev(d, e) for d, e in plane_peers]
    peers += [at((z + d) % NZ, x, core) for d in range(1, NZ)]
    peers += [(me, (hd + d) % nh) for d in range(1, nh)]
    for dev in peers:
        pl.semaphore_signal(barrier, inc=1, device_id=dev, device_id_type=pl.DeviceIdType.MESH)

    packt[...] = jnp.zeros((w, n), F32)
    packt[0:heads, :] = ldt[...]
    packt[8:8 + LV_ALL, :] = lwt[...]
    packt[15:16, :] = sgt[...].astype(F32)
    pk = packt[...].T
    rows = lax.broadcasted_iota(jnp.int32, (n, n), 0)
    cols = lax.broadcasted_iota(jnp.int32, (n, n), 1)
    tri = (cols <= rows).astype(BF16)
    p1 = pk.astype(BF16)
    rest = pk - p1.astype(F32)
    p2 = rest.astype(BF16)
    p3 = (rest - p2.astype(F32)).astype(BF16)
    cum = mm(tri, p1, 1, 0) + mm(tri, p2, 1, 0) + mm(tri, p3, 1, 0)
    total = cum[n - 1:n, :]
    seg = pk[:, 15:16]
    own_end = pk[n - 1:n, 15:16]
    lane1 = lax.broadcasted_iota(jnp.int32, (1, w), 1)
    own_row = jnp.where(lane1 == heads, jnp.broadcast_to(own_end, (1, w)), total)
    pb[r0] = jnp.broadcast_to(own_row, (8, w))

    pl.semaphore_wait(barrier, len(peers))

    def g1(j):
        d, e = plane_peers[j]
        return cp(pb.at[r0], pb.at[r0], s_g.at[j], r_g.at[j], plane_dev(d, e))

    def g3(d):
        return cp(zt.at[z], zt.at[z], s_g.at[6 + d], r_g.at[6 + d], at((z + d) % NZ, x, core))

    for j in range(7):
        g1(j).start()
    sw = jnp.exp(total - cum) * (seg == own_end).astype(F32)
    for h in range(heads):
        swcol[h] = jnp.broadcast_to(sw[:, h:h + 1], (n, w))

    def own(i):
        return 2 * i + core

    def other(i):
        return 2 * i + 1 - core

    def f1_send(h):
        return cp(st.at[h], rf.at[0, h], s_1.at[h], r_1.at[h], partner)

    def head_cols(h):
        return pl.ds(pl.multiple_of(h * w, w), w)

    bring(0).wait()
    bring(1).wait()

    def make_state(h):
        vt = v[:, head_cols(h)].T
        st[h] = mm(left(vt, 1), right(k[:, head_cols(h)] * swcol[h], 0), 1, 0)

    def state_other(i):
        make_state(other(i))
        f1_send(other(i)).start()

    def state_own(i):
        make_state(own(i))

        @pl.when(core == 0)
        def _():
            f1_send(own(i)).start()

    loop(half, state_other)
    for j in range(7):
        g1(j).wait_recv()
    sub = lax.broadcasted_iota(jnp.int32, (8, w), 0)
    lane8 = lax.broadcasted_iota(jnp.int32, (8, w), 1)
    plane = jnp.zeros((8, w), F32)
    for r in range(8):
        plane = jnp.where(sub == r, pb[r], plane)
    zt[z] = plane
    for d in range(1, NZ):
        g3(d).start()

    def tools(tbl, idx):
        def row(c):
            return jnp.sum(jnp.where(idx == c, tbl, 0.0), axis=0, keepdims=True)

        def span(lo, hi):
            inside_span = jnp.where((idx > lo) & (idx <= hi), tbl, 0.0)
            return jnp.exp(jnp.minimum(jnp.sum(inside_span, axis=0, keepdims=True), 0.0))

        def same(a, b):
            return (row(a)[:, heads:heads + 1] == row(b)[:, heads:heads + 1]).astype(F32)

        return row, span, same

    def spread(vec):
        m = jnp.where(lane8 == sub, jnp.broadcast_to(vec, (8, w)), 0.0)
        return jnp.broadcast_to(jnp.sum(m, axis=1, keepdims=True), (8, w))

    row, span, same = tools(plane, sub)
    for l, low in ((0, 2 * x), (1, 4 * (x // 2) + 1)):
        up = low + (1 << l)
        bfac[l] = spread(span(low, up) * same(low, up))
    for j in range(NX):
        pfac[j] = spread(span(2 * j + 1, 7) * same(2 * j + 1, 7))

    def bf(l, h):
        return bfac[l, pl.ds(h, 1), :]

    def gf(l, h):
        return gfac[l, pl.ds(h, 1), :]

    def pf(j, h):
        return pfac[j, pl.ds(h, 1), :]

    loop(half, state_own)

    def f2_send(i):
        return cp(tt.at[i], rf.at[1, own(i)], s_x.at[0, i], r_x.at[0, i], at(z, (x + 1) % NX, core))

    def rs_send(d):
        i = (x + d) % NX
        return cp(tt.at[i], rsb.at[x], s_rs.at[d - 1], r_rs.at[d - 1], at(z, i, core))

    def rs_in(d):
        j = (x + NX - d) % NX
        return cp(tt.at[x], rsb.at[j], s_rs.at[d - 1], r_rs.at[d - 1], at(z, j, core))

    def f1(i):
        h = own(i)
        f1_send(h).wait_recv()
        b = bf(0, h)
        u = core == 1
        tt[i] = jnp.where(u, 1.0, b) * st[h] + jnp.where(u, b, 1.0) * rf[0, h]

    loop(half, f1)
    for d in (2, 1, 3):
        rs_send(d).start()

    @pl.when(x % 2 == 0)
    def _():
        loop(half, lambda i: f2_send(i).start())

    for h in range(heads):
        cumcol[h] = jnp.broadcast_to(cum[:, h:h + 1], (n, w))
    for l in range(LV_ALL):
        lwcol[l] = jnp.broadcast_to(pk[:, 8 + l:9 + l], (n, w))
    cumt[...] = cum.T
    segrow = packt[15:16, :]
    vis = (cols <= rows) & (jnp.broadcast_to(seg, (n, n)) == jnp.broadcast_to(segrow, (n, n)))
    bias[...] = jnp.where(vis, 0.0, -1e30)
    for l in range(LV_ALL):
        lev[l] = jnp.zeros((n, w), F32)

    for d in (1, 3, 2):
        rs_in(d).wait_recv()
    acc = pf(x, r0) * tt[x]
    for d in range(1, NX):
        j = (x + NX - d) % NX
        acc = acc + pf(j, r0) * rsb[j]
    zs[0] = acc

    def z4_send():
        return cp(zs.at[0], rf.at[3, r0], s_z.at[0], r_z.at[0], at((z + 1) % NZ, x, core))

    def z5_send(d):
        return cp(zs.at[1], rf.at[4, r0], s_z.at[d], r_z.at[1], at((z + d) % NZ, x, core))

    def z6_send(d):
        return cp(zs.at[2], rf.at[5, r0], s_z.at[2 + d], r_z.at[2], at((z + d) % NZ, x, core))

    @pl.when(z % 2 == 0)
    def _():
        z4_send().start()

    for d in range(1, NZ):
        g3(d).wait_recv()
    row, span, same = tools(zt[...].reshape(8 * NZ, w), lax.broadcasted_iota(jnp.int32, (8 * NZ, w), 0))
    for l in range(LV):
        hs = 1 << l
        low = (me // (2 * hs)) * (2 * hs) + hs - 1
        gfac[l] = spread(span(low, me - 1) * same(low, me - 1) * bits[l].astype(F32))
        if l in (3, 4):
            bfac[l] = spread(span(low, low + hs) * same(low, low + hs))
    prev_end = row(me - 1)[:, heads:heads + 1]
    ecum = jnp.exp(cum) * (seg == prev_end).astype(F32)
    for h in range(heads):
        ecol[h] = jnp.broadcast_to(ecum[:, h:h + 1], (n, w))

    def gp_send(l, i):
        return cp(gs.at[l, other(i)], gr.at[l - 1, i], s_p.at[l - 1, i], r_p.at[l - 1, i], partner)

    def make_g(h, l):
        lhs = left(o[:, head_cols(h)].T, 1)
        qe = q[:, head_cols(h)] * ecol[h]
        a = jnp.concatenate([qe * lwcol[l + 1], qe * lwcol[l + 2]], axis=1)
        both = mm(lhs, right(a, 0), 1, 0)
        gs[l, h] = both[:, :w] * gf(l, h)
        gs[l + 1, h] = both[:, w:] * gf(l + 1, h)

    def g_other(l):
        def one(i):
            make_g(other(i), l)
            for m in (l + 1, l):
                if m:
                    @pl.when(bits[m] == 1)
                    def _():
                        gp_send(m, i).start()

        return one

    def g_own(l):
        def one(i):
            make_g(own(i), l)

        return one

    def gsum(l, i):
        return gs[l, own(i)] + gr[l - 1, i]

    def bs_send(m, d):
        i = (x + d) % NX
        return cp(gx.at[m, i], rsg.at[m, x], s_bs.at[m, d - 1], r_bs.at[m, d - 1], at(z, i, core))

    def bs_in(m, d):
        j = (x + NX - d) % NX
        return cp(gx.at[m, x], rsg.at[m, j], s_bs.at[m, d - 1], r_bs.at[m, d - 1], at(z, j, core))

    def bs_out(m):
        @pl.when(bits[3 + m] == 1)
        def _():
            def one(i):
                gp_send(3 + m, i).wait_recv()
                gx[m, i] = gsum(3 + m, i)

            loop(half, one)
            for d in (2, 1, 3):
                bs_send(m, d).start()

    def bs_sum(m):
        for d in (1, 3, 2):
            bs_in(m, d).wait_recv()
        t = gx[m, x]
        for d in range(1, NX):
            t = t + rsg[m, (x + NX - d) % NX]
        gp[m] = t

    bring(2).wait()
    bring(3).wait()
    loop(half, g_other(4))
    loop(half, g_own(4))
    bs_out(2)

    @pl.when(z % 2 == 1)
    def _():
        z4_send().wait_recv()
        zs[1] = bf(3, r0) * rf[3, r0] + zs[0]

        @pl.when((z // 2) % 2 == 0)
        def _():
            z5_send(2).start()
            z5_send(1).start()

    loop(half, g_other(2))
    loop(half, g_own(2))
    bs_out(1)
    bs_out(0)

    @pl.when(z == 3)
    def _():
        z5_send(1).wait_recv()
        zs[2] = bf(4, r0) * rf[4, r0] + zs[1]
        for d in (4, 3, 2, 1):
            z6_send(d).start()

    def b6_send():
        return cp(gp.at[2], rz6.at[z % 4], s_bz.at[0], r_bz.at[z % 4], at(3, x, core))

    def b6_in(j):
        return cp(gp.at[2], rz6.at[j], s_bz.at[0], r_bz.at[j], at(4 + j, x, core))

    def b5_send():
        return cp(za.at[1], rz5.at[z % 2], s_bz.at[1], r_bz.at[4 + z % 2], at(4 * (z // 4) + 1, x, core))

    def b5_in(j):
        return cp(za.at[1], rz5.at[j], s_bz.at[1], r_bz.at[4 + j], at((z + 1 + j) % NZ, x, core))

    def b4_send():
        return cp(za.at[0], rz4, s_bz.at[2], r_bz.at[6], at((z + NZ - 1) % NZ, x, core))

    @pl.when(z >= 4)
    def _():
        bs_sum(2)
        b6_send().start()

    @pl.when(bits[4] == 1)
    def _():
        bs_sum(1)

        @pl.when(z != 3)
        def _():
            za[1] = gp[1]
            b5_send().start()

    @pl.when(z % 2 == 1)
    def _():
        bs_sum(0)

        @pl.when(z == 7)
        def _():
            za[0] = gp[0]
            b4_send().start()

    def ag_send(m, d):
        slot = rf.at[3 + m, r0]
        return cp(slot, slot, s_ag.at[m, d - 1], r_ag.at[m, d - 1], at(z, (x + d) % NX, core))

    def ag_in(m, d):
        slot = rf.at[3 + m, own((x + NX - d) % NX)]
        return cp(slot, slot, s_ag.at[m, d - 1], r_ag.at[m, d - 1], at(z, (x + NX - d) % NX, core))

    def fwd(l, i):
        slot = rf.at[l, own(i)]
        return cp(slot, slot, s_f.at[l - 1, i], r_f.at[l - 1, i], partner)

    def fwd_in(l, i):
        slot = rf.at[l, other(i)]
        return cp(slot, slot, s_f.at[l - 1, i], r_f.at[l - 1, i], partner)

    def hand_round(m):
        for d in (2, 1, 3):
            ag_send(m, d).start()
        fwd(3 + m, x).start()

    def hand_on(m):
        for d in (1, 3, 2):
            ag_in(m, d).wait_recv()
            fwd(3 + m, (x + NX - d) % NX).start()

    @pl.when(z % 2 == 1)
    def _():
        hand_round(0)

    @pl.when(bits[4] == 1)
    def _():
        @pl.when(z != 3)
        def _():
            z5_send(1).wait_recv()

        hand_round(1)

    def f3_send(src, i):
        return cp(src, rf.at[2, own(i)], s_x.at[1, i], r_x.at[1, i], at(z, (x + 1) % NX, core))

    @pl.when(x % 2 == 1)
    def _():
        def one(i):
            h = own(i)
            f2_send(i).wait_recv()
            fwd(1, i).start()

            @pl.when(x == 1)
            def _():
                t01[i] = bf(1, h) * rf[1, h] + tt[i]
                f3_send(t01.at[i], i).start()

        loop(half, one)

    loop(half, g_other(0))
    loop(half, g_own(0))

    def b3_send(i):
        return cp(m3.at[i], r3.at[i], s_m.at[0, i], r_m.at[0, i], at(z, (x + NX - 1) % NX, core))

    def b2_send(i):
        return cp(m2.at[i], r2.at[i], s_m.at[1, i], r_m.at[1, i], at(z, (x + NX - 1) % NX, core))

    @pl.when(x == 3)
    def _():
        def one(i):
            gp_send(2, i).wait_recv()
            m3[i] = gsum(2, i)
            b3_send(i).start()

        loop(half, one)

    def b1_early(i):
        return cp(gs.at[0, 2 * i], rl.at[2 * i], s_b1.at[i], r_b1.at[i], partner)

    @pl.when(core == 1)
    def _():
        loop(half, lambda i: b1_early(i).start())

    @pl.when(x == 2)
    def _():
        def one(i):
            f3_send(t01.at[i], i).wait_recv()
            f3_send(rf.at[2, own(i)], i).start()
            fwd(2, i).start()
            gp_send(2, i).wait_recv()
            b3_send(i).wait_recv()
            m3[i] = gsum(2, i) + r3[i]
            b3_send(i).start()

        loop(half, one)

    def inside(h):
        hc = head_cols(h)
        qh, kh, vh, oh = q[:, hc], k[:, hc], v[:, hc], o[:, hc]
        cc = cumcol[h]
        gap = jnp.concatenate([cc, cc], axis=1) - cumt[pl.ds(h, 1), :]
        within = jnp.exp(jnp.minimum(gap, 0.0) + bias[...])
        sc = mm(left(qh, 1), right(kh, 1), 1, 1)
        go = mm(left(oh, 1), right(vh, 1), 1, 1)
        lw = lwcol[0]
        wt = within * jnp.concatenate([lw, lw], axis=1)
        prod = within * sc * go
        lev[0] += prod[:, :w] + prod[:, w:]
        a = wt * sc
        b = wt * go
        dq[:, hc] = mm(left(b, 1), right(kh, 0), 1, 0)
        dv[:, hc] = mm(left(a.T, 1), right(oh, 0), 1, 0)
        dk[:, hc] = mm(left(b.T, 1), right(qh, 0), 1, 0)

    loop(half, inside)

    @pl.when(bits[3] == 1)
    def _():
        hand_on(0)

    @pl.when(bits[4] == 1)
    def _():
        hand_on(1)

    @pl.when(z == 3)
    def _():
        for j in range(4):
            b6_in(j).wait_recv()
        t = rz6[0] + rz6[1] + rz6[2] + rz6[3]
        za[1] = gp[1] + bf(4, r0) * t
        b5_send().start()
        za[0] = gp[0] + bf(3, r0) * t
        b4_send().start()
        db[x] = t

    @pl.when(z % 4 == 1)
    def _():
        for j in range(2):
            b5_in(j).wait_recv()
        t = rz5[0] + rz5[1]
        za[0] = gp[0] + bf(3, r0) * t
        b4_send().start()
        db[x] = t

    @pl.when(z == 7)
    def _():
        db[x] = jnp.zeros((w, w), F32)

    @pl.when(x % 2 == 1)
    def _():
        def one(i):
            gp_send(1, i).wait_recv()

            @pl.when(x == 1)
            def _():
                b3_send(i).wait_recv()
                m2[i] = gsum(1, i) + bf(1, own(i)) * r3[i]

            @pl.when(x == 3)
            def _():
                m2[i] = gsum(1, i)
                f3_send(t01.at[i], i).wait_recv()
                fwd(2, i).start()

            b2_send(i).start()

        loop(half, one)

    @pl.when(z >= 4)
    def _():
        z6_send(1).wait_recv()
        hand_round(2)

    @pl.when(z % 2 == 0)
    def _():
        b4_send().wait_recv()
        db[x] = rz4[...]

    def d_send(d):
        return cp(db.at[x], db.at[x], s_d.at[d - 1], r_d.at[d - 1], at(z, (x + d) % NX, core))

    def d_in(d):
        slot = db.at[(x + NX - d) % NX]
        return cp(slot, slot, s_d.at[d - 1], r_d.at[d - 1], at(z, (x + NX - d) % NX, core))

    for d in (2, 1, 3):
        d_send(d).start()
    loop(half, lambda i: inside(half + i))

    @pl.when(z >= 4)
    def _():
        hand_on(2)

    @pl.when(core == 1)
    def _():
        loop(half, lambda i: f1_send(2 * i).wait_recv())

    for l in range(1, 5):
        @pl.when(bits[l] == 1)
        def _():
            loop(half, lambda i: fwd_in(l, i).wait_recv())

    for d in (1, 3, 2):
        d_in(d).wait_recv()

    @pl.when(x % 2 == 0)
    def _():
        loop(half, lambda i: b2_send(i).wait_recv())

    def b1_up(i):
        return cp(ml.at[i], rl.at[own(i)], s_b1.at[half + i], r_b1.at[half + i], partner)

    def b1_up_in(i):
        return cp(ml.at[i], rl.at[other(i)], s_b1.at[half + i], r_b1.at[half + i], partner)

    def b1(i):
        h = own(i)
        t = pf(x, h) * db[i]
        extra = jnp.where(x == 1, r3[i], jnp.where(x == 3, 0.0, r2[i]))
        lam = t + extra

        @pl.when(core == 1)
        def _():
            ml[i] = bf(0, h) * lam + gs[0, h]
            rl[h] = lam

        @pl.when(core == 0)
        def _():
            ml[i] = lam
            b1_early(i).wait_recv()
            rl[h] = bf(0, h) * lam + rl[h]

        b1_up(i).start()

    loop(half, b1)

    def put(j, h):
        src, dst = ((dq, dq_hbm), (dk, dk_hbm), (dv, dv_hbm))[j]
        hc = head_cols(h)
        return pltpu.make_async_copy(src.at[:, hc], dst.at[:, hc], s_out.at[j, h])

    @pl.when(bits[5] == 1)
    def _():
        loop(half, lambda i: fwd_in(5, i).wait_recv())

    def levels(h):
        hc = head_cols(h)
        oh = left(o[:, hc], 1)
        qh = q[:, hc]
        e = ecol[h]
        acc = dq[:, hc]
        for l in range(0, LV, 2):
            pair = []
            for m in (l, l + 1):
                pair.append(jnp.where(bits[m] == 1, rf[m, h] * gf(m, h), 0.0))
            back = mm(oh, right(jnp.concatenate(pair, axis=1), 0), 1, 0)
            for m in (l, l + 1):
                part = e * back[:, (m - l) * w:(m - l + 1) * w]
                lev[m + 1] += qh * part
                acc = acc + lwcol[m + 1] * part
        dq[:, hc] = acc
        put(0, h).start()

    def sources(h):
        hc = head_cols(h)
        g = rl[h]
        s = swcol[h]
        dk[:, hc] += s * mm(left(v[:, hc], 1), right(g, 0), 1, 0)
        put(1, h).start()
        dv[:, hc] += s * mm(left(k[:, hc], 1), right(g, 1), 1, 1)
        put(2, h).start()

    loop(heads, levels)

    lanes = lax.broadcasted_iota(jnp.int32, (n, w), 1)
    acc = jnp.zeros((n, w), F32)
    for l in range(LV_ALL):
        acc = jnp.where(lanes == l, jnp.sum(lev[l], axis=1, keepdims=True), acc)
    hb[hd] = acc.T[:8, :]

    def h_send(d):
        return cp(hb.at[hd], hb.at[hd], s_h.at[d - 1], r_h.at[d - 1], (me, (hd + d) % nh))

    for d in range(1, nh):
        h_send(d).start()
    loop(half, lambda i: b1_up_in(i).wait_recv())
    loop(heads, sources)
    for d in range(1, nh):
        h_send(d).wait_recv()
    tot = hb[0] + hb[1] + hb[2] + hb[3]
    glt[...] = tot[:LV_ALL, :]

    for j in range(3):
        loop(heads, lambda h: put(j, h).wait())
    for d in range(1, nh):
        h_send(d).wait_send()
    for j in range(7):
        g1(j).wait_send()
    for d in range(1, NZ):
        g3(d).wait_send()
    loop(half, lambda i: f1_send(other(i)).wait_send())

    @pl.when(core == 0)
    def _():
        loop(half, lambda i: f1_send(own(i)).wait_send())

    @pl.when(core == 1)
    def _():
        loop(half, lambda i: b1_early(i).wait_send())

    for d in range(1, NX):
        rs_send(d).wait_send()
        d_send(d).wait_send()

    @pl.when(x % 2 == 0)
    def _():
        loop(half, lambda i: f2_send(i).wait_send())

    @pl.when((x == 1) | (x == 2))
    def _():
        loop(half, lambda i: f3_send(t01.at[i], i).wait_send())

    @pl.when(x >= 2)
    def _():
        loop(half, lambda i: b3_send(i).wait_send())

    @pl.when(x % 2 == 1)
    def _():
        loop(half, lambda i: b2_send(i).wait_send())

    loop(half, lambda i: b1_up(i).wait_send())
    for l in range(1, LV):
        @pl.when(bits[l] == 1)
        def _():
            loop(half, lambda i: fwd(l, i).wait_send())
            loop(half, lambda i: gp_send(l, i).wait_send())

    for m in range(3):
        @pl.when(bits[3 + m] == 1)
        def _():
            for d in range(1, NX):
                bs_send(m, d).wait_send()
                ag_send(m, d).wait_send()

    @pl.when(z % 2 == 0)
    def _():
        z4_send().wait_send()

    @pl.when(z % 4 == 1)
    def _():
        z5_send(1).wait_send()
        z5_send(2).wait_send()

    @pl.when(z == 3)
    def _():
        for d in range(1, 5):
            z6_send(d).wait_send()

    @pl.when(z >= 4)
    def _():
        b6_send().wait_send()

    @pl.when(bits[4] == 1)
    def _():
        b5_send().wait_send()

    @pl.when(z % 2 == 1)
    def _():
        b4_send().wait_send()


def on_device(queries, key_input, value_input, grad_output, log_decay, level_weight, segment):
    n, heads = log_decay.shape
    width = queries.shape[1]
    w = 128
    half = heads // 2
    dma = pltpu.SemaphoreType.DMA

    def mem(*shape):
        return pltpu.VMEM(shape, F32)

    scratch = [mem(n, width) for _ in range(7)] + [mem(w, n)]
    scratch += [mem(heads, n, w), mem(heads, n, w), mem(heads, n, w), mem(LV_ALL, n, w),
                mem(w, n), mem(n, n), mem(LV, 8, w), mem(LV, 8, w), mem(NX, 8, w), mem(LV_ALL, n, w)]
    scratch += [mem(8, 8, w), mem(NZ, 8, w), mem(heads, w, w), mem(LV, heads, w, w),
                mem(half, w, w), mem(half, w, w), mem(NX, w, w), mem(3, w, w),
                mem(LV, heads, w, w), mem(LV - 1, half, w, w), mem(3, half, w, w), mem(3, NX, w, w),
                mem(3, w, w), mem(2, w, w), mem(4, w, w), mem(2, w, w), mem(w, w), mem(NX, w, w)]
    scratch += [mem(half, w, w) for _ in range(4)] + [mem(heads, w, w), mem(half, w, w), mem(4, 8, n)]
    scratch += [dma((4,)), dma((3, heads))]
    for a, b in (((14,), (14,)), ((heads,), (heads,)), ((3,), (3,)), ((2, half), (2, half)), ((7,), (3,)),
                 ((3, 3), (3, 3)), ((LV - 1, half), (LV - 1, half)), ((LV - 1, half), (LV - 1, half)),
                 ((3, 3), (3, 3)), ((3,), (7,)), ((3,), (3,)), ((2, half), (2, half)),
                 ((heads,), (heads,)), ((3,), (3,))):
        scratch += [dma(a), dma(b)]
    vm = pl.BlockSpec(memory_space=pltpu.VMEM)
    hbm = pl.BlockSpec(memory_space=pl.ANY)
    out = jax.ShapeDtypeStruct((n, width), F32)
    dq, dk, dv, glt = pl.pallas_call(
        kernel,
        out_shape=(out, out, out, jax.ShapeDtypeStruct((LV_ALL, n), F32)),
        in_specs=[vm] * 3 + [hbm] * 4,
        out_specs=(hbm, hbm, hbm, vm),
        scratch_shapes=scratch,
        compiler_params=pltpu.CompilerParams(
            collective_id=0, has_side_effects=True, vmem_limit_bytes=60 << 20),
    )(log_decay.T, level_weight.T, segment[None, :], queries, key_input, value_input, grad_output)
    return dq, dk, dv, glt.T


def solution(mesh):
    in_specs = (
        P("seq", "head"),
        P("seq", "head"),
        P("seq", "head"),
        P("seq", "head"),
        P("seq", "head"),
        P("seq", None),
        P("seq"),
    )
    out_specs = (P("seq", "head"), P("seq", "head"), P("seq", "head"), P("seq", None))
    return jax.shard_map(
        on_device, mesh=mesh, in_specs=in_specs, out_specs=out_specs, check_vma=False
    )
```

```python
import jax
import jax.numpy as jnp
from jax import lax
from jax.experimental import pallas as pl
from jax.experimental.pallas import tpu as pltpu
from jax.sharding import PartitionSpec as P

F32 = jnp.float32
BF16 = jnp.bfloat16
NZ, NX = 8, 4
LV_ALL = 7
LV = 6


def split(a):
    hi = a.astype(BF16)
    return hi, (a - hi.astype(F32)).astype(BF16)


def left(a, axis):
    hi, lo = split(a)
    return jnp.concatenate([hi, hi, lo], axis=axis)


def right(a, axis):
    hi, lo = split(a)
    return jnp.concatenate([hi, lo, hi], axis=axis)


def mm(a, b, ca, cb):
    return lax.dot_general(a, b, (((ca,), (cb,)), ((), ())), preferred_element_type=F32)


def loop(n, fn):
    def body(i, carry):
        fn(i)
        return carry

    lax.fori_loop(0, n, body, 0)


def kernel(ldt, lwt, sgt, q_hbm, k_hbm, v_hbm, o_hbm, dq_hbm, dk_hbm, dv_hbm, glt,
           q, k, v, o, dq, dk, dv, packt,
           cumcol, ecol, swcol, lwcol, cumt, bias, bfac, gfac, hfac, pfac, lev,
           pb, zt, st, rf, tt, t01, rsb, zs, gs, gr, gx, rsg, gp, za, rz6, rz5, rz4, db,
           gxx, rsx, lo, dp, ge, rl, ml, hb, olhs,
           s_in, s_out, s_g, r_g, s_1, r_1, s_rs, r_rs, s_x, r_x, s_z, r_z, s_ag, r_ag, s_f, r_f, s_p, r_p,
           s_bs, r_bs, s_bz, r_bz, s_d, r_d, s_m, r_m, s_b1, r_b1, s_h, r_h):
    n, heads, w = q.shape[0], swcol.shape[0], 128
    half = heads // 2
    me = lax.axis_index("seq")
    hd = lax.axis_index("head")
    nh = 4
    core = me % 2
    x = (me // 2) % NX
    z = me // (2 * NX)
    bits = [core, x % 2, x // 2, z % 2, (z // 2) % 2, z // 4]
    r0 = x * 2 + core

    def at(zz, xx, cc):
        return ((zz * NX + xx) * 2 + cc, hd)

    partner = at(z, x, 1 - core)

    def cp(src, dst, ss, rs, dev):
        return pltpu.make_async_remote_copy(
            src_ref=src, dst_ref=dst, send_sem=ss, recv_sem=rs,
            device_id=dev, device_id_type=pl.DeviceIdType.MESH)

    def bring(j):
        src, dst = ((k_hbm, k), (v_hbm, v), (o_hbm, o), (q_hbm, q))[j]
        return pltpu.make_async_copy(src, dst, s_in.at[j])

    for j in range(4):
        bring(j).start()

    barrier = pltpu.get_barrier_semaphore()
    plane_peers = [(d, e) for d in range(NX) for e in range(2) if (d, e) != (0, 0)]

    def plane_dev(d, e):
        return at(z, (x + d) % NX, (core + e) % 2)

    peers = [plane_dev(d, e) for d, e in plane_peers]
    peers += [at((z + d) % NZ, x, core) for d in range(1, NZ)]
    peers += [(me, (hd + d) % nh) for d in range(1, nh)]
    for dev in peers:
        pl.semaphore_signal(barrier, inc=1, device_id=dev, device_id_type=pl.DeviceIdType.MESH)

    packt[...] = jnp.zeros((w, n), F32)
    packt[0:heads, :] = ldt[...]
    packt[8:8 + LV_ALL, :] = lwt[...]
    packt[15:16, :] = sgt[...].astype(F32)
    pk = packt[...].T
    rows = lax.broadcasted_iota(jnp.int32, (n, n), 0)
    cols = lax.broadcasted_iota(jnp.int32, (n, n), 1)
    tri = (cols <= rows).astype(BF16)
    p1 = pk.astype(BF16)
    rest = pk - p1.astype(F32)
    p2 = rest.astype(BF16)
    p3 = (rest - p2.astype(F32)).astype(BF16)
    cum = mm(tri, p1, 1, 0) + mm(tri, p2, 1, 0) + mm(tri, p3, 1, 0)
    total = cum[n - 1:n, :]
    seg = pk[:, 15:16]
    own_end = pk[n - 1:n, 15:16]
    lane1 = lax.broadcasted_iota(jnp.int32, (1, w), 1)
    own_row = jnp.where(lane1 == heads, jnp.broadcast_to(own_end, (1, w)), total)
    own_row = jnp.where(lane1 == heads + 1, jnp.broadcast_to(pk[0:1, 15:16], (1, w)), own_row)
    pb[r0] = jnp.broadcast_to(own_row, (8, w))

    pl.semaphore_wait(barrier, len(peers))

    def g1(j):
        d, e = plane_peers[j]
        return cp(pb.at[r0], pb.at[r0], s_g.at[j], r_g.at[j], plane_dev(d, e))

    def g3(d):
        return cp(zt.at[z], zt.at[z], s_g.at[6 + d], r_g.at[6 + d], at((z + d) % NZ, x, core))

    for j in range(7):
        g1(j).start()
    sw = jnp.exp(total - cum) * (seg == own_end).astype(F32)
    for h in range(heads):
        swcol[h] = jnp.broadcast_to(sw[:, h:h + 1], (n, w))

    def own(i):
        return 2 * i + core

    def other(i):
        return 2 * i + 1 - core

    def f1_send(h):
        return cp(st.at[h], rf.at[0, h], s_1.at[h], r_1.at[h], partner)

    def head_cols(h):
        return pl.ds(pl.multiple_of(h * w, w), w)

    bring(0).wait()
    bring(1).wait()

    def make_state(h):
        vt = v[:, head_cols(h)].T
        st[h] = mm(left(vt, 1), right(k[:, head_cols(h)] * swcol[h], 0), 1, 0)

    def state_other(i):
        make_state(other(i))
        f1_send(other(i)).start()

    def state_own(i):
        make_state(own(i))

        @pl.when(core == 0)
        def _():
            f1_send(own(i)).start()

    loop(half, state_other)
    loop(half, state_own)
    first = pk[0:1, 15:16]
    ecum = jnp.exp(cum) * (seg == first).astype(F32)
    for h in range(heads):
        ecol[h] = jnp.broadcast_to(ecum[:, h:h + 1], (n, w))
    for l in range(LV_ALL):
        lwcol[l] = jnp.broadcast_to(pk[:, 8 + l:9 + l], (n, w))

    def gp_send(l, i):
        return cp(gs.at[l, other(i)], gr.at[l - 1, i], s_p.at[l - 1, i], r_p.at[l - 1, i], partner)

    def make_g(h, l):
        if l == 4:
            olhs[h] = left(o[:, head_cols(h)].T, 1)
        lhs = olhs[h]
        qe = q[:, head_cols(h)] * ecol[h]
        a = jnp.concatenate([qe * lwcol[l + 1], qe * lwcol[l + 2]], axis=1)
        both = mm(lhs, right(a, 0), 1, 0)
        gs[l, h] = both[:, :w]
        gs[l + 1, h] = both[:, w:]

    def g_other(l):
        def one(i):
            make_g(other(i), l)
            for m in (l + 1, l):
                if m:
                    @pl.when(bits[m] == 1)
                    def _():
                        gp_send(m, i).start()

        return one

    def g_own(l):
        def one(i):
            make_g(own(i), l)

        return one

    bring(2).wait()
    bring(3).wait()
    loop(half, g_other(4))
    for j in range(7):
        g1(j).wait_recv()
    sub = lax.broadcasted_iota(jnp.int32, (8, w), 0)
    lane8 = lax.broadcasted_iota(jnp.int32, (8, w), 1)
    plane = jnp.zeros((8, w), F32)
    for r in range(8):
        plane = jnp.where(sub == r, pb[r], plane)
    zt[z] = plane
    for d in range(1, NZ):
        g3(d).start()

    def tools(tbl, idx):
        def row(c):
            return jnp.sum(jnp.where(idx == c, tbl, 0.0), axis=0, keepdims=True)

        def span(lo, hi):
            inside_span = jnp.where((idx > lo) & (idx <= hi), tbl, 0.0)
            return jnp.exp(jnp.minimum(jnp.sum(inside_span, axis=0, keepdims=True), 0.0))

        def same(a, b):
            return (row(a)[:, heads:heads + 1] == row(b)[:, heads:heads + 1]).astype(F32)

        return row, span, same

    def spread(vec):
        m = jnp.where(lane8 == sub, jnp.broadcast_to(vec, (8, w)), 0.0)
        return jnp.broadcast_to(jnp.sum(m, axis=1, keepdims=True), (8, w))

    row, span, same = tools(plane, sub)
    for l, low in ((0, 2 * x), (1, 1)):
        up = low + (1 << l)
        bfac[l] = spread(span(low, up) * same(low, up))
    for j in range(NX):
        pfac[j] = spread(span(2 * j + 1, 7) * same(2 * j + 1, 7))

    def bf(l, h):
        return bfac[l, pl.ds(h, 1), :]

    def gf(l, h):
        return gfac[l, pl.ds(h, 1), :]

    def pf(j, h):
        return pfac[j, pl.ds(h, 1), :]

    def rs_send(d):
        i = (x + d) % NX
        return cp(tt.at[i], rsb.at[x], s_rs.at[d - 1], r_rs.at[d - 1], at(z, i, core))

    def rs_in(d):
        j = (x + NX - d) % NX
        return cp(tt.at[x], rsb.at[j], s_rs.at[d - 1], r_rs.at[d - 1], at(z, j, core))

    def f1(i):
        h = own(i)
        f1_send(h).wait_recv()
        b = bf(0, h)
        u = core == 1
        tt[i] = jnp.where(u, 1.0, b) * st[h] + jnp.where(u, b, 1.0) * rf[0, h]

    loop(half, f1)
    for d in (2, 1, 3):
        rs_send(d).start()

    loop(half, g_own(4))
    loop(half, g_other(2))
    for h in range(heads):
        cumcol[h] = jnp.broadcast_to(cum[:, h:h + 1], (n, w))
    cumt[...] = cum.T
    segrow = packt[15:16, :]
    vis = (cols <= rows) & (jnp.broadcast_to(seg, (n, n)) == jnp.broadcast_to(segrow, (n, n)))
    bias[...] = jnp.where(vis, 0.0, -1e30)
    for l in range(LV_ALL):
        lev[l] = jnp.zeros((n, w), F32)

    loop(half, g_own(2))

    for d in (1, 3, 2):
        rs_in(d).wait_recv()
    rsb[x] = tt[x]
    acc = pf(0, r0) * rsb[0]
    for j in range(1, NX):
        acc = acc + pf(j, r0) * rsb[j]
    zs[0] = acc

    def z4_send():
        return cp(zs.at[0], rf.at[3, r0], s_z.at[0], r_z.at[0], at((z + 1) % NZ, x, core))

    def z5_send(d):
        return cp(zs.at[1], rf.at[4, r0], s_z.at[d], r_z.at[1], at((z + d) % NZ, x, core))

    def z6_send(d):
        return cp(zs.at[2], rf.at[5, r0], s_z.at[2 + d], r_z.at[2], at((z + d) % NZ, x, core))

    @pl.when(z % 2 == 0)
    def _():
        z4_send().start()

    for d in range(1, NZ):
        g3(d).wait_recv()
    row, span, same = tools(zt[...].reshape(8 * NZ, w), lax.broadcasted_iota(jnp.int32, (8 * NZ, w), 0))
    def starts(r):
        c = z * 2 * NX + r
        return (row(c)[:, heads + 1:heads + 2] == row(c - 1)[:, heads:heads + 1]).astype(F32)

    for l in range(LV):
        hs = 1 << l
        low = (me // (2 * hs)) * (2 * hs) + hs - 1
        prev = me - 1
        gfac[l] = spread(span(low, prev) * same(low, prev) * starts(r0) * bits[l].astype(F32))
        if l:
            other_prev = me - 2 * core
            hfac[l] = spread(span(low, other_prev) * same(low, other_prev) * starts(r0 + 1 - 2 * core) * bits[l].astype(F32))
        if l in (3, 4):
            bfac[l] = spread(span(low, low + hs) * same(low, low + hs))
    def gsum(l, i):
        return gs[l, own(i)] * gf(l, own(i)) + gr[l - 1, i] * hfac[l, pl.ds(own(i), 1), :]

    def bs_send(m, d):
        i = (x + d) % NX
        return cp(gx.at[m, i], rsg.at[m, x], s_bs.at[m, d - 1], r_bs.at[m, d - 1], at(z, i, core))

    def bs_in(m, d):
        j = (x + NX - d) % NX
        return cp(gx.at[m, x], rsg.at[m, j], s_bs.at[m, d - 1], r_bs.at[m, d - 1], at(z, j, core))

    def bs_out(m):
        @pl.when(bits[3 + m] == 1)
        def _():
            def one(i):
                gp_send(3 + m, i).wait_recv()
                gx[m, i] = gsum(3 + m, i)

            loop(half, one)
            for d in (2, 1, 3):
                bs_send(m, d).start()

    def bs_sum(m):
        for d in (1, 3, 2):
            bs_in(m, d).wait_recv()
        t = gx[m, x]
        for d in range(1, NX):
            t = t + rsg[m, (x + NX - d) % NX]
        gp[m] = t

    bs_out(2)
    bs_out(1)
    bs_out(0)
    loop(half, g_other(0))
    loop(half, g_own(0))

    def ag_send(m, d):
        slot = rf.at[3 + m, r0]
        return cp(slot, slot, s_ag.at[m, d - 1], r_ag.at[m, d - 1], at(z, (x + d) % NX, core))

    def ag_in(m, d):
        slot = rf.at[3 + m, own((x + NX - d) % NX)]
        return cp(slot, slot, s_ag.at[m, d - 1], r_ag.at[m, d - 1], at(z, (x + NX - d) % NX, core))

    def fwd(l, i):
        slot = rf.at[l, own(i)]
        return cp(slot, slot, s_f.at[l - 1, i], r_f.at[l - 1, i], partner)

    def fwd_in(l, i):
        slot = rf.at[l, other(i)]
        return cp(slot, slot, s_f.at[l - 1, i], r_f.at[l - 1, i], partner)

    def hand_round(m):
        for d in (2, 1, 3):
            ag_send(m, d).start()
        fwd(3 + m, x).start()

    def hand_on(m):
        for d in (1, 3, 2):
            ag_in(m, d).wait_recv()
            fwd(3 + m, (x + NX - d) % NX).start()

    @pl.when(z % 2 == 1)
    def _():
        z4_send().wait_recv()
        zs[1] = bf(3, r0) * rf[3, r0] + zs[0]

        @pl.when((z // 2) % 2 == 0)
        def _():
            z5_send(2).start()
            z5_send(1).start()

    @pl.when(z % 2 == 1)
    def _():
        hand_round(0)

    def bx_send(c, l, d):
        i = (x + d) % NX
        return cp(gxx.at[l - 1, i], rsx.at[c], s_m.at[l - 1, d - 1], r_m.at[c], at(z, i, core))

    def bx_in(c, l):
        return cp(gxx.at[l - 1, x], rsx.at[c], s_m.at[l - 1, 0], r_m.at[c], at(z, x, 1 - core))

    b_plan = ((1, 1), (3, 1), (2, 2), (3, 2))
    for c in (2, 3, 0, 1):
        frm, l = b_plan[c]

        @pl.when(x == frm)
        def _():
            def one(i):
                gp_send(l, i).wait_recv()
                gxx[l - 1, i] = gsum(l, i)

            loop(half, one)
            rsx[c] = gxx[l - 1, x]
            for d in (2, 1, 3):
                bx_send(c, l, d).start()

    t01[...] = bf(1, r0) * rsb[0] + rsb[1]
    x_plan = ((1, 1, 0), (3, 1, 2), (2, 2, None), (3, 2, None))

    def fx_send(c):
        to, l, j = x_plan[c]
        src = t01 if j is None else rsb.at[j]
        return cp(src, rf.at[l, r0], s_x.at[c], r_x.at[l - 1, (to + NX - x + 3) % NX], at(z, to, core))

    def fx_in(l, d):
        j = (x + NX - d) % NX
        return cp(t01, rf.at[l, own(j)], s_x.at[0], r_x.at[l - 1, d - 1], at(z, j, core))

    for c in range(4):
        to, l, j = x_plan[c]

        @pl.when(x == to)
        def _():
            rf[l, r0] = t01[...] if j is None else rsb[j]

        @pl.when(x != to)
        def _():
            fx_send(c).start()

    def b6_send():
        return cp(gp.at[2], rz6.at[z % 4], s_bz.at[0], r_bz.at[z % 4], at(3, x, core))

    def b6_in(j):
        return cp(gp.at[2], rz6.at[j], s_bz.at[0], r_bz.at[j], at(4 + j, x, core))

    def b5_send():
        return cp(za.at[1], rz5.at[z % 2], s_bz.at[1], r_bz.at[4 + z % 2], at(4 * (z // 4) + 1, x, core))

    def b5_in(j):
        return cp(za.at[1], rz5.at[j], s_bz.at[1], r_bz.at[4 + j], at((z + 1 + j) % NZ, x, core))

    def b4_send():
        return cp(za.at[0], rz4, s_bz.at[2], r_bz.at[6], at((z + NZ - 1) % NZ, x, core))

    @pl.when(z >= 4)
    def _():
        bs_sum(2)
        b6_send().start()

    @pl.when(z == 3)
    def _():
        z5_send(1).wait_recv()
        zs[2] = bf(4, r0) * rf[4, r0] + zs[1]
        for d in (4, 3, 2, 1):
            z6_send(d).start()

    @pl.when(bits[4] == 1)
    def _():
        @pl.when(z != 3)
        def _():
            z5_send(1).wait_recv()

        hand_round(1)

    def b1_early(i):
        return cp(ge.at[i], rl.at[2 * i], s_b1.at[i], r_b1.at[i], partner)

    @pl.when(core == 1)
    def _():
        def one(i):
            ge[i] = gs[0, 2 * i] * gf(0, 2 * i)
            b1_early(i).start()

        loop(half, one)

    def inside(h):
        hc = head_cols(h)
        qh, kh, vh, oh = q[:, hc], k[:, hc], v[:, hc], o[:, hc]
        cc = cumcol[h]
        gap = jnp.concatenate([cc, cc], axis=1) - cumt[pl.ds(h, 1), :]
        within = jnp.exp(jnp.minimum(gap, 0.0) + bias[...])
        sc = mm(left(qh, 1), right(kh, 1), 1, 1)
        go = mm(left(oh, 1), right(vh, 1), 1, 1)
        lw = lwcol[0]
        wt = within * jnp.concatenate([lw, lw], axis=1)
        prod = within * sc * go
        lev[0] += prod[:, :w] + prod[:, w:]
        a = wt * sc
        b = wt * go
        dq[:, hc] = mm(left(b, 1), right(kh, 0), 1, 0)
        dv[:, hc] = mm(left(a.T, 1), right(oh, 0), 1, 0)
        dk[:, hc] = mm(left(b.T, 1), right(qh, 0), 1, 0)

    def d_send(d):
        return cp(lo.at[(x + d) % NX], db.at[x], s_d.at[d - 1], r_d.at[d - 1], at(z, (x + d) % NX, core))

    def d_in(d):
        return cp(lo.at[x], db.at[(x + NX - d) % NX], s_d.at[d - 1], r_d.at[d - 1], at(z, (x + NX - d) % NX, core))

    def b1_up(i):
        return cp(ml.at[i], rl.at[own(i)], s_b1.at[half + i], r_b1.at[half + i], partner)

    def b1_up_in(i):
        return cp(ml.at[i], rl.at[other(i)], s_b1.at[half + i], r_b1.at[half + i], partner)

    def b1(i):
        h = own(i)
        lam = db[i]

        @pl.when(core == 1)
        def _():
            ml[i] = bf(0, h) * lam + gs[0, h] * gf(0, h)
            rl[h] = lam

        @pl.when(core == 0)
        def _():
            ml[i] = lam
            b1_early(i).wait_recv()
            rl[h] = bf(0, h) * lam + rl[h]

        b1_up(i).start()

    def put(j, h):
        src, dst = ((dq, dq_hbm), (dk, dk_hbm), (dv, dv_hbm))[j]
        hc = head_cols(h)
        return pltpu.make_async_copy(src.at[:, hc], dst.at[:, hc], s_out.at[j, h])

    def levels(pairs, last):
        def one(h):
            hc = head_cols(h)
            oh = left(o[:, hc], 1)
            qh = q[:, hc]
            e = ecol[h]
            acc = dq[:, hc]
            for l in pairs:
                pair = []
                for m in (l, l + 1):
                    pair.append(jnp.where(bits[m] == 1, rf[m, h] * gf(m, h), 0.0))
                back = mm(oh, right(jnp.concatenate(pair, axis=1), 0), 1, 0)
                for m in (l, l + 1):
                    part = e * back[:, (m - l) * w:(m - l + 1) * w]
                    lev[m + 1] += qh * part
                    acc = acc + lwcol[m + 1] * part
            dq[:, hc] = acc
            if last:
                put(0, h).start()

        loop(heads, one)

    def sources(h):
        hc = head_cols(h)
        g = rl[h]
        s = swcol[h]
        dk[:, hc] += s * mm(left(v[:, hc], 1), right(g, 0), 1, 0)
        put(1, h).start()
        dv[:, hc] += s * mm(left(k[:, hc], 1), right(g, 1), 1, 1)
        put(2, h).start()

    def h_send(d):
        return cp(hb.at[hd], hb.at[hd], s_h.at[d - 1], r_h.at[d - 1], (me, (hd + d) % nh))

    def level_sums():
        lanes = lax.broadcasted_iota(jnp.int32, (n, w), 1)
        acc = jnp.zeros((n, w), F32)
        for l in range(LV_ALL):
            acc = jnp.where(lanes == l, jnp.sum(lev[l], axis=1, keepdims=True), acc)
        hb[hd] = acc.T[:8, :]
        for d in range(1, nh):
            h_send(d).start()

    def x_blocks():
        def fx_all(l):
            fwd(l, x).start()
            for d in (1, 3, 2):
                fx_in(l, d).wait_recv()
                fwd(l, (x + NX - d) % NX).start()

        @pl.when(x % 2 == 1)
        def _():
            fx_all(1)

        @pl.when(x >= 2)
        def _():
            fx_all(2)

    def from_partner(levels_in):
        for l in levels_in:
            @pl.when(bits[l] == 1)
            def _():
                loop(half, lambda i: fwd_in(l, i).wait_recv())

    def plane_gradient():
        @pl.when(z % 2 == 0)
        def _():
            b4_send().wait_recv()
            dp[...] = rz4[...]

        for c in range(4):
            frm, l = b_plan[c]

            @pl.when(x != frm)
            def _():
                bx_in(c, l).wait_recv()

        t = dp[...]
        both = rsx[2] + rsx[3]
        lo[0] = pf(0, r0) * t + rsx[0] + bf(1, r0) * both
        lo[1] = pf(1, r0) * t + both
        lo[2] = pf(2, r0) * t + rsx[1]
        lo[3] = pf(3, r0) * t
        db[x] = lo[x]
        for d in (2, 1, 3):
            d_send(d).start()

    def finish_sources():
        for d in (1, 3, 2):
            d_in(d).wait_recv()

        loop(half, b1)
        loop(half, lambda i: b1_up_in(i).wait_recv())
        loop(heads, sources)

    def blocks_45():
        @pl.when(bits[3] == 1)
        def _():
            hand_on(0)

        @pl.when(bits[4] == 1)
        def _():
            hand_on(1)

    def chain_down():
        for j in range(2):
            b5_in(j).wait_recv()
        t = rz5[0] + rz5[1]
        za[0] = gp[0] + bf(3, r0) * t
        b4_send().start()
        dp[...] = t


    @pl.when(z == 7)
    def _():
        dp[...] = jnp.zeros((w, w), F32)

    loop(half, inside)
    @pl.when(bits[4] == 1)
    def _():
        bs_sum(1)

        @pl.when(z != 3)
        def _():
            za[1] = gp[1]
            b5_send().start()

    @pl.when(z % 2 == 1)
    def _():
        bs_sum(0)

        @pl.when(z == 7)
        def _():
            za[0] = gp[0]
            b4_send().start()


    @pl.when(core == 1)
    def _():
        loop(half, lambda i: f1_send(2 * i).wait_recv())

    @pl.when(z < 4)
    def _():
        @pl.when(z == 3)
        def _():
            for j in range(4):
                b6_in(j).wait_recv()
            t = rz6[0] + rz6[1] + rz6[2] + rz6[3]
            za[1] = gp[1] + bf(4, r0) * t
            b5_send().start()
            za[0] = gp[0] + bf(3, r0) * t
            b4_send().start()
            dp[...] = t

        blocks_45()
        x_blocks()
        loop(half, lambda i: inside(half + i))
        from_partner(range(1, 5))
        levels((0, 2), False)

        @pl.when(z == 1)
        def _():
            chain_down()

        levels((4,), True)
        level_sums()
        plane_gradient()
        finish_sources()

    @pl.when(z >= 4)
    def _():
        @pl.when(z == 5)
        def _():
            chain_down()

        z6_send(1).wait_recv()
        hand_round(2)
        loop(half, lambda i: inside(half + i))
        plane_gradient()
        x_blocks()
        blocks_45()
        from_partner(range(1, 5))
        levels((0, 2), False)
        hand_on(2)
        from_partner((5,))
        levels((4,), True)
        level_sums()
        finish_sources()

    for d in range(1, nh):
        h_send(d).wait_recv()
    tot = hb[0] + hb[1] + hb[2] + hb[3]
    glt[...] = tot[:LV_ALL, :]

    for j in range(3):
        loop(heads, lambda h: put(j, h).wait())
    for d in range(1, nh):
        h_send(d).wait_send()
    for j in range(7):
        g1(j).wait_send()
    for d in range(1, NZ):
        g3(d).wait_send()
    loop(half, lambda i: f1_send(other(i)).wait_send())

    @pl.when(core == 0)
    def _():
        loop(half, lambda i: f1_send(own(i)).wait_send())

    @pl.when(core == 1)
    def _():
        loop(half, lambda i: b1_early(i).wait_send())

    for d in range(1, NX):
        rs_send(d).wait_send()
        d_send(d).wait_send()

    for c in range(4):
        @pl.when(x != x_plan[c][0])
        def _():
            fx_send(c).wait_send()

        frm, l = b_plan[c]

        @pl.when(x == frm)
        def _():
            for d in range(1, NX):
                bx_send(c, l, d).wait_send()

    loop(half, lambda i: b1_up(i).wait_send())
    for l in range(1, LV):
        @pl.when(bits[l] == 1)
        def _():
            loop(half, lambda i: fwd(l, i).wait_send())
            loop(half, lambda i: gp_send(l, i).wait_send())

    for m in range(3):
        @pl.when(bits[3 + m] == 1)
        def _():
            for d in range(1, NX):
                bs_send(m, d).wait_send()
                ag_send(m, d).wait_send()

    @pl.when(z % 2 == 0)
    def _():
        z4_send().wait_send()

    @pl.when(z % 4 == 1)
    def _():
        z5_send(1).wait_send()
        z5_send(2).wait_send()

    @pl.when(z == 3)
    def _():
        for d in range(1, 5):
            z6_send(d).wait_send()

    @pl.when(z >= 4)
    def _():
        b6_send().wait_send()

    @pl.when(bits[4] == 1)
    def _():
        b5_send().wait_send()

    @pl.when(z % 2 == 1)
    def _():
        b4_send().wait_send()


def on_device(queries, key_input, value_input, grad_output, log_decay, level_weight, segment):
    n, heads = log_decay.shape
    width = queries.shape[1]
    w = 128
    half = heads // 2
    dma = pltpu.SemaphoreType.DMA

    def mem(*shape):
        return pltpu.VMEM(shape, F32)

    scratch = [mem(n, width) for _ in range(7)] + [mem(w, n)]
    scratch += [mem(heads, n, w), mem(heads, n, w), mem(heads, n, w), mem(LV_ALL, n, w),
                mem(w, n), mem(n, n), mem(LV, 8, w), mem(LV, 8, w), mem(LV, 8, w), mem(NX, 8, w), mem(LV_ALL, n, w)]
    scratch += [mem(8, 8, w), mem(NZ, 8, w), mem(heads, w, w), mem(LV, heads, w, w),
                mem(half, w, w), mem(w, w), mem(NX, w, w), mem(3, w, w),
                mem(LV, heads, w, w), mem(LV - 1, half, w, w), mem(3, half, w, w), mem(3, NX, w, w),
                mem(3, w, w), mem(2, w, w), mem(4, w, w), mem(2, w, w), mem(w, w), mem(NX, w, w)]
    scratch += [mem(2, half, w, w), mem(4, w, w), mem(NX, w, w), mem(w, w), mem(half, w, w)] + [mem(heads, w, w), mem(half, w, w), mem(4, 8, n),
                pltpu.VMEM((heads, w, 3 * n), BF16)]
    scratch += [dma((4,)), dma((3, heads))]
    for a, b in (((14,), (14,)), ((heads,), (heads,)), ((3,), (3,)), ((4,), (2, 3)), ((7,), (3,)),
                 ((3, 3), (3, 3)), ((LV - 1, half), (LV - 1, half)), ((LV - 1, half), (LV - 1, half)),
                 ((3, 3), (3, 3)), ((3,), (7,)), ((3,), (3,)), ((2, 3), (4,)),
                 ((heads,), (heads,)), ((3,), (3,))):
        scratch += [dma(a), dma(b)]
    vm = pl.BlockSpec(memory_space=pltpu.VMEM)
    hbm = pl.BlockSpec(memory_space=pl.ANY)
    out = jax.ShapeDtypeStruct((n, width), F32)
    dq, dk, dv, glt = pl.pallas_call(
        kernel,
        out_shape=(out, out, out, jax.ShapeDtypeStruct((LV_ALL, n), F32)),
        in_specs=[vm] * 3 + [hbm] * 4,
        out_specs=(hbm, hbm, hbm, vm),
        scratch_shapes=scratch,
        compiler_params=pltpu.CompilerParams(
            collective_id=0, has_side_effects=True, vmem_limit_bytes=60 << 20),
    )(log_decay.T, level_weight.T, segment[None, :], queries, key_input, value_input, grad_output)
    return dq, dk, dv, glt.T


def solution(mesh):
    in_specs = (
        P("seq", "head"),
        P("seq", "head"),
        P("seq", "head"),
        P("seq", "head"),
        P("seq", "head"),
        P("seq", None),
        P("seq"),
    )
    out_specs = (P("seq", "head"), P("seq", "head"), P("seq", "head"), P("seq", None))
    return jax.shard_map(
        on_device, mesh=mesh, in_specs=in_specs, out_specs=out_specs, check_vma=False
    )
```

```python
import jax
import jax.numpy as jnp
from jax import lax
from jax.experimental import pallas as pl
from jax.experimental.pallas import tpu as pltpu
from jax.sharding import PartitionSpec as P

F32 = jnp.float32
BF16 = jnp.bfloat16
NZ, NX = 8, 4
LV_ALL = 7
LV = 6


def split(a):
    hi = a.astype(BF16)
    return hi, (a - hi.astype(F32)).astype(BF16)


def left(a, axis):
    hi, lo = split(a)
    return jnp.concatenate([hi, hi, lo], axis=axis)


def right(a, axis):
    hi, lo = split(a)
    return jnp.concatenate([hi, lo, hi], axis=axis)


def mm(a, b, ca, cb):
    return lax.dot_general(a, b, (((ca,), (cb,)), ((), ())), preferred_element_type=F32)


def loop(n, fn):
    def body(i, carry):
        fn(i)
        return carry

    lax.fori_loop(0, n, body, 0)


def kernel(ldt, lwt, sgt, q_hbm, k_hbm, v_hbm, o_hbm, dq, dk, dv, glt,
           q, k, v, o, packt,
           cumcol, ecol, swcol, lwcol, cumt, bias, bfac, gfac, hfac, pfac, lev,
           pb, zt, st, rf, tt, t01, rsb, zs, gs, gr, gx, rsg, gp, za, rz6, rz5, rz4, db,
           gxx, rsx, lo, dp, ge, rl, ml, hb, olhs,
           s_in, s_g, r_g, s_1, r_1, s_rs, r_rs, s_x, r_x, s_z, r_z, s_ag, r_ag, s_f, r_f, s_p, r_p,
           s_bs, r_bs, s_bz, r_bz, s_d, r_d, s_m, r_m, s_b1, r_b1, s_h, r_h):
    n, heads, w = q.shape[0], swcol.shape[0], 128
    half = heads // 2
    me = lax.axis_index("seq")
    hd = lax.axis_index("head")
    nh = 4
    core = me % 2
    x = (me // 2) % NX
    z = me // (2 * NX)
    bits = [core, x % 2, x // 2, z % 2, (z // 2) % 2, z // 4]
    r0 = x * 2 + core

    def at(zz, xx, cc):
        return ((zz * NX + xx) * 2 + cc, hd)

    partner = at(z, x, 1 - core)

    def cp(src, dst, ss, rs, dev):
        return pltpu.make_async_remote_copy(
            src_ref=src, dst_ref=dst, send_sem=ss, recv_sem=rs,
            device_id=dev, device_id_type=pl.DeviceIdType.MESH)

    def bring(j):
        src, dst = ((k_hbm, k), (v_hbm, v), (o_hbm, o), (q_hbm, q))[j]
        return pltpu.make_async_copy(src, dst, s_in.at[j])

    for j in range(4):
        bring(j).start()

    barrier = pltpu.get_barrier_semaphore()
    plane_peers = [(d, e) for d in range(NX) for e in range(2) if (d, e) != (0, 0)]

    def plane_dev(d, e):
        return at(z, (x + d) % NX, (core + e) % 2)

    peers = [plane_dev(d, e) for d, e in plane_peers]
    peers += [at((z + d) % NZ, x, core) for d in range(1, NZ)]
    peers += [at((z + e) % NZ, (x + d) % NX, core) for d in range(1, NX) for e in (1, NZ - 1)]
    peers += [(me, (hd + d) % nh) for d in range(1, nh)]
    for dev in peers:
        pl.semaphore_signal(barrier, inc=1, device_id=dev, device_id_type=pl.DeviceIdType.MESH)

    packt[...] = jnp.zeros((w, n), F32)
    packt[0:heads, :] = ldt[...]
    packt[8:8 + LV_ALL, :] = lwt[...]
    packt[15:16, :] = sgt[...].astype(F32)
    pk = packt[...].T
    rows = lax.broadcasted_iota(jnp.int32, (n, n), 0)
    cols = lax.broadcasted_iota(jnp.int32, (n, n), 1)
    tri = (cols <= rows).astype(BF16)
    p1 = pk.astype(BF16)
    rest = pk - p1.astype(F32)
    p2 = rest.astype(BF16)
    p3 = (rest - p2.astype(F32)).astype(BF16)
    cum = mm(tri, p1, 1, 0) + mm(tri, p2, 1, 0) + mm(tri, p3, 1, 0)
    total = cum[n - 1:n, :]
    seg = pk[:, 15:16]
    own_end = pk[n - 1:n, 15:16]
    lane1 = lax.broadcasted_iota(jnp.int32, (1, w), 1)
    own_row = jnp.where(lane1 == heads, jnp.broadcast_to(own_end, (1, w)), total)
    own_row = jnp.where(lane1 == heads + 1, jnp.broadcast_to(pk[0:1, 15:16], (1, w)), own_row)
    pb[r0] = jnp.broadcast_to(own_row, (8, w))

    sw = jnp.exp(total - cum) * (seg == own_end).astype(F32)
    for h in range(heads):
        swcol[h] = jnp.broadcast_to(sw[:, h:h + 1], (n, w))

    def own(i):
        return 2 * i + core

    def other(i):
        return 2 * i + 1 - core

    def f1_send(h):
        return cp(st.at[h], rf.at[0, h], s_1.at[h], r_1.at[h], partner)

    def head_cols(h):
        return pl.ds(pl.multiple_of(h * w, w), w)

    bring(0).wait()
    bring(1).wait()

    def make_state(h):
        vt = v[:, head_cols(h)].T
        st[h] = mm(left(vt, 1), right(k[:, head_cols(h)] * swcol[h], 0), 1, 0)

    def state_other(i):
        make_state(other(i))

    def state_own(i):
        make_state(own(i))

        @pl.when(core == 0)
        def _():
            f1_send(own(i)).start()

    first = pk[0:1, 15:16]
    ecum = jnp.exp(cum) * (seg == first).astype(F32)
    for h in range(heads):
        ecol[h] = jnp.broadcast_to(ecum[:, h:h + 1], (n, w))
    for l in range(LV_ALL):
        lwcol[l] = jnp.broadcast_to(pk[:, 8 + l:9 + l], (n, w))


    loop(half, state_other)
    pl.semaphore_wait(barrier, len(peers))
    def g1(j):
        d, e = plane_peers[j]
        return cp(pb.at[r0], pb.at[r0], s_g.at[j], r_g.at[j], plane_dev(d, e))

    def g3(d):
        return cp(zt.at[z], zt.at[z], s_g.at[6 + d], r_g.at[6 + d], at((z + d) % NZ, x, core))

    for j in range(7):
        g1(j).start()
    loop(half, lambda i: f1_send(other(i)).start())
    loop(half, state_own)
    def gp_send(l, i):
        return cp(gs.at[l, other(i)], gr.at[l - 1, i], s_p.at[l - 1, i], r_p.at[l - 1, i], partner)

    def make_g(h, l):
        if l == 4:
            olhs[h] = left(o[:, head_cols(h)].T, 1)
        lhs = olhs[h]
        qe = q[:, head_cols(h)] * ecol[h]
        a = jnp.concatenate([qe * lwcol[l + 1], qe * lwcol[l + 2]], axis=1)
        both = mm(lhs, right(a, 0), 1, 0)
        gs[l, h] = both[:, :w]
        gs[l + 1, h] = both[:, w:]

    def g_other(l):
        def one(i):
            make_g(other(i), l)
            for m in (l + 1, l):
                if m:
                    @pl.when(bits[m] == 1)
                    def _():
                        gp_send(m, i).start()

        return one

    def g_own(l):
        def one(i):
            make_g(own(i), l)

        return one

    bring(2).wait()
    bring(3).wait()
    loop(half, g_other(4))
    loop(half, g_own(4))
    for j in range(7):
        g1(j).wait_recv()
    sub = lax.broadcasted_iota(jnp.int32, (8, w), 0)
    lane8 = lax.broadcasted_iota(jnp.int32, (8, w), 1)
    plane = jnp.zeros((8, w), F32)
    for r in range(8):
        plane = jnp.where(sub == r, pb[r], plane)
    zt[z] = plane
    for d in range(1, NZ):
        g3(d).start()

    def tools(tbl, idx):
        def row(c):
            return jnp.sum(jnp.where(idx == c, tbl, 0.0), axis=0, keepdims=True)

        def span(lo, hi):
            inside_span = jnp.where((idx > lo) & (idx <= hi), tbl, 0.0)
            return jnp.exp(jnp.minimum(jnp.sum(inside_span, axis=0, keepdims=True), 0.0))

        def same(a, b):
            return (row(a)[:, heads:heads + 1] == row(b)[:, heads:heads + 1]).astype(F32)

        return row, span, same

    def spread(vec):
        m = jnp.where(lane8 == sub, jnp.broadcast_to(vec, (8, w)), 0.0)
        return jnp.broadcast_to(jnp.sum(m, axis=1, keepdims=True), (8, w))

    row, span, same = tools(plane, sub)
    for l, low in ((0, 2 * x), (1, 1)):
        up = low + (1 << l)
        bfac[l] = spread(span(low, up) * same(low, up))
    for j in range(NX):
        pfac[j] = spread(span(2 * j + 1, 7) * same(2 * j + 1, 7))

    def bf(l, h):
        return bfac[l, pl.ds(h, 1), :]

    def gf(l, h):
        return gfac[l, pl.ds(h, 1), :]

    def pf(j, h):
        return pfac[j, pl.ds(h, 1), :]

    def rs_send(d):
        i = (x + d) % NX
        return cp(tt.at[i], rsb.at[x], s_rs.at[d - 1], r_rs.at[d - 1], at(z, i, core))

    def rs_in(d):
        j = (x + NX - d) % NX
        return cp(tt.at[x], rsb.at[j], s_rs.at[d - 1], r_rs.at[d - 1], at(z, j, core))

    def f1(i):
        h = own(i)
        f1_send(h).wait_recv()
        b = bf(0, h)
        u = core == 1
        tt[i] = jnp.where(u, 1.0, b) * st[h] + jnp.where(u, b, 1.0) * rf[0, h]

    loop(half, f1)
    for d in (2, 1, 3):
        rs_send(d).start()

    loop(half, g_other(2))
    for h in range(heads):
        cumcol[h] = jnp.broadcast_to(cum[:, h:h + 1], (n, w))
    cumt[...] = cum.T
    segrow = packt[15:16, :]
    vis = (cols <= rows) & (jnp.broadcast_to(seg, (n, n)) == jnp.broadcast_to(segrow, (n, n)))
    bias[...] = jnp.where(vis, 0.0, -1e30)
    for l in range(LV_ALL):
        lev[l] = jnp.zeros((n, w), F32)

    loop(half, g_own(2))
    loop(half, g_other(0))
    loop(half, g_own(0))

    for d in (1, 3, 2):
        rs_in(d).wait_recv()
    rsb[x] = tt[x]
    acc = pf(0, r0) * rsb[0]
    for j in range(1, NX):
        acc = acc + pf(j, r0) * rsb[j]
    zs[0] = acc

    def z4_send():
        return cp(zs.at[0], rf.at[3, r0], s_z.at[0], r_z.at[0], at((z + 1) % NZ, x, core))

    def z5_send(d):
        return cp(zs.at[1], rf.at[4, r0], s_z.at[d], r_z.at[1], at((z + d) % NZ, x, core))

    def z6_send(d):
        return cp(zs.at[2], rf.at[5, r0], s_z.at[2 + d], r_z.at[2], at((z + d) % NZ, x, core))

    def z4_round(d):
        return cp(zs.at[0], rf.at[3, r0], s_ag.at[0, d - 1], r_ag.at[0, d - 1], at((z + 1) % NZ, (x + d) % NX, core))

    @pl.when(z % 2 == 0)
    def _():
        z4_send().start()
        for d in (2, 1, 3):
            z4_round(d).start()

    for d in range(1, NZ):
        g3(d).wait_recv()
    row, span, same = tools(zt[...].reshape(8 * NZ, w), lax.broadcasted_iota(jnp.int32, (8 * NZ, w), 0))
    def starts(r):
        c = z * 2 * NX + r
        return (row(c)[:, heads + 1:heads + 2] == row(c - 1)[:, heads:heads + 1]).astype(F32)

    for l in range(LV):
        hs = 1 << l
        low = (me // (2 * hs)) * (2 * hs) + hs - 1
        prev = me - 1
        gfac[l] = spread(span(low, prev) * same(low, prev) * starts(r0) * bits[l].astype(F32))
        if l:
            other_prev = me - 2 * core
            hfac[l] = spread(span(low, other_prev) * same(low, other_prev) * starts(r0 + 1 - 2 * core) * bits[l].astype(F32))
        if l in (3, 4):
            bfac[l] = spread(span(low, low + hs) * same(low, low + hs))
    def gsum(l, i):
        return gs[l, own(i)] * gf(l, own(i)) + gr[l - 1, i] * hfac[l, pl.ds(own(i), 1), :]

    def bs_send(m, d):
        i = (x + d) % NX
        to = z if m else (z + NZ - 1) % NZ
        return cp(gx.at[m, i], rsg.at[m, x], s_bs.at[m, (d + 3) % 4], r_bs.at[m, (d + 3) % 4], at(to, i, core))

    def bs_in(m, d):
        j = (x + NX - d) % NX
        frm = z if m else (z + 1) % NZ
        return cp(gx.at[m, x], rsg.at[m, j], s_bs.at[m, (d + 3) % 4], r_bs.at[m, (d + 3) % 4], at(frm, j, core))

    def bs_out(m):
        @pl.when(bits[3 + m] == 1)
        def _():
            def one(i):
                gp_send(3 + m, i).wait_recv()
                gx[m, i] = gsum(3 + m, i)

            loop(half, one)
            for d in (2, 1, 3) if m else (2, 1, 3, 0):
                bs_send(m, d).start()

    def bs_sum(m):
        for d in (1, 3, 2):
            bs_in(m, d).wait_recv()
        t = gx[m, x]
        for d in range(1, NX):
            t = t + rsg[m, (x + NX - d) % NX]
        gp[m] = t

    def inside(h):
        hc = head_cols(h)
        qh, kh, vh, oh = q[:, hc], k[:, hc], v[:, hc], o[:, hc]
        cc = cumcol[h]
        gap = jnp.concatenate([cc, cc], axis=1) - cumt[pl.ds(h, 1), :]
        within = jnp.exp(jnp.minimum(gap, 0.0) + bias[...])
        sc = mm(left(qh, 1), right(kh, 1), 1, 1)
        go = mm(left(oh, 1), right(vh, 1), 1, 1)
        lw = lwcol[0]
        wt = within * jnp.concatenate([lw, lw], axis=1)
        prod = within * sc * go
        lev[0] += prod[:, :w] + prod[:, w:]
        a = wt * sc
        b = wt * go
        dq[:, hc] = mm(left(b, 1), right(kh, 0), 1, 0)
        dv[:, hc] = mm(left(a.T, 1), right(oh, 0), 1, 0)
        dk[:, hc] = mm(left(b.T, 1), right(qh, 0), 1, 0)

    bs_out(2)
    bs_out(1)
    bs_out(0)
    loop(2, inside)

    def ag_send(m, d):
        slot = rf.at[3 + m, r0]
        return cp(slot, slot, s_ag.at[m, d - 1], r_ag.at[m, d - 1], at(z, (x + d) % NX, core))

    def ag_in(m, d):
        slot = rf.at[3 + m, own((x + NX - d) % NX)]
        return cp(slot, slot, s_ag.at[m, d - 1], r_ag.at[m, d - 1], at(z, (x + NX - d) % NX, core))

    def fwd(l, i):
        slot = rf.at[l, own(i)]
        return cp(slot, slot, s_f.at[l - 1, i], r_f.at[l - 1, i], partner)

    def fwd_in(l, i):
        slot = rf.at[l, other(i)]
        return cp(slot, slot, s_f.at[l - 1, i], r_f.at[l - 1, i], partner)

    def hand_round(m):
        for d in (2, 1, 3):
            ag_send(m, d).start()
        fwd(3 + m, x).start()

    def hand_on(m):
        for d in (1, 3, 2):
            ag_in(m, d).wait_recv()
            fwd(3 + m, (x + NX - d) % NX).start()

    @pl.when(z % 2 == 1)
    def _():
        z4_send().wait_recv()
        zs[1] = bf(3, r0) * rf[3, r0] + zs[0]

        @pl.when((z // 2) % 2 == 0)
        def _():
            z5_send(2).start()
            z5_send(1).start()

    @pl.when(z % 2 == 1)
    def _():
        fwd(3, x).start()

    def bx_send(c, l, d):
        i = (x + d) % NX
        return cp(gxx.at[l - 1, i], rsx.at[c], s_m.at[l - 1, d - 1], r_m.at[c], at(z, i, core))

    def bx_in(c, l):
        return cp(gxx.at[l - 1, x], rsx.at[c], s_m.at[l - 1, 0], r_m.at[c], at(z, x, 1 - core))

    b_plan = ((1, 1), (3, 1), (2, 2), (3, 2))
    for c in (2, 3, 0, 1):
        frm, l = b_plan[c]

        @pl.when(x == frm)
        def _():
            def one(i):
                gp_send(l, i).wait_recv()
                gxx[l - 1, i] = gsum(l, i)

            loop(half, one)
            rsx[c] = gxx[l - 1, x]
            for d in (2, 1, 3):
                bx_send(c, l, d).start()

    t01[...] = bf(1, r0) * rsb[0] + rsb[1]
    x_plan = ((1, 1, 0), (3, 1, 2), (2, 2, None), (3, 2, None))

    def fx_send(c):
        to, l, j = x_plan[c]
        src = t01 if j is None else rsb.at[j]
        return cp(src, rf.at[l, r0], s_x.at[c], r_x.at[l - 1, (to + NX - x + 3) % NX], at(z, to, core))

    def fx_in(l, d):
        j = (x + NX - d) % NX
        return cp(t01, rf.at[l, own(j)], s_x.at[0], r_x.at[l - 1, d - 1], at(z, j, core))

    for c in range(4):
        to, l, j = x_plan[c]

        @pl.when(x == to)
        def _():
            rf[l, r0] = t01[...] if j is None else rsb[j]

        @pl.when(x != to)
        def _():
            fx_send(c).start()

    def b6_send():
        return cp(gp.at[2], rz6.at[z % 4], s_bz.at[0], r_bz.at[z % 4], at(3, x, core))

    def b6_in(j):
        return cp(gp.at[2], rz6.at[j], s_bz.at[0], r_bz.at[j], at(4 + j, x, core))

    def b5_send():
        return cp(za.at[1], rz5.at[z % 2], s_bz.at[1], r_bz.at[4 + z % 2], at(4 * (z // 4) + 1, x, core))

    def b5_in(j):
        return cp(za.at[1], rz5.at[j], s_bz.at[1], r_bz.at[4 + j], at((z + 1 + j) % NZ, x, core))

    def b4_send():
        return cp(za.at[0], rz4, s_bz.at[2], r_bz.at[6], at((z + NZ - 1) % NZ, x, core))

    @pl.when(z >= 4)
    def _():
        bs_sum(2)
        b6_send().start()

    loop(2, lambda i: inside(2 + i))

    @pl.when(z == 3)
    def _():
        z5_send(1).wait_recv()
        zs[2] = bf(4, r0) * rf[4, r0] + zs[1]
        for d in (4, 3, 2, 1):
            z6_send(d).start()

    @pl.when(bits[4] == 1)
    def _():
        @pl.when(z != 3)
        def _():
            z5_send(1).wait_recv()

        hand_round(1)

    def b1_early(i):
        return cp(ge.at[i], rl.at[2 * i], s_b1.at[i], r_b1.at[i], partner)

    @pl.when(core == 1)
    def _():
        def one(i):
            ge[i] = gs[0, 2 * i] * gf(0, 2 * i)
            b1_early(i).start()

        loop(half, one)

    def d_send(d):
        return cp(lo.at[(x + d) % NX], db.at[x], s_d.at[d - 1], r_d.at[d - 1], at(z, (x + d) % NX, core))

    def d_in(d):
        return cp(lo.at[x], db.at[(x + NX - d) % NX], s_d.at[d - 1], r_d.at[d - 1], at(z, (x + NX - d) % NX, core))

    def b1_up(i):
        return cp(ml.at[i], rl.at[own(i)], s_b1.at[half + i], r_b1.at[half + i], partner)

    def b1_up_in(i):
        return cp(ml.at[i], rl.at[other(i)], s_b1.at[half + i], r_b1.at[half + i], partner)

    def b1(i):
        h = own(i)
        lam = db[i]

        @pl.when(core == 1)
        def _():
            ml[i] = bf(0, h) * lam + gs[0, h] * gf(0, h)
            rl[h] = lam

        @pl.when(core == 0)
        def _():
            ml[i] = lam
            b1_early(i).wait_recv()
            rl[h] = bf(0, h) * lam + rl[h]

        b1_up(i).start()

    def levels(pairs):
        def one(h):
            hc = head_cols(h)
            oh = left(o[:, hc], 1)
            qh = q[:, hc]
            e = ecol[h]
            acc = dq[:, hc]
            for l in pairs:
                pair = []
                for m in (l, l + 1):
                    pair.append(jnp.where(bits[m] == 1, rf[m, h] * gf(m, h), 0.0))
                back = mm(oh, right(jnp.concatenate(pair, axis=1), 0), 1, 0)
                for m in (l, l + 1):
                    part = e * back[:, (m - l) * w:(m - l + 1) * w]
                    lev[m + 1] += qh * part
                    acc = acc + lwcol[m + 1] * part
            dq[:, hc] = acc

        loop(heads, one)

    def sources(h):
        hc = head_cols(h)
        g = rl[h]
        s = swcol[h]
        dk[:, hc] += s * mm(left(v[:, hc], 1), right(g, 0), 1, 0)
        dv[:, hc] += s * mm(left(k[:, hc], 1), right(g, 1), 1, 1)

    def h_send(d):
        return cp(hb.at[hd], hb.at[hd], s_h.at[d - 1], r_h.at[d - 1], (me, (hd + d) % nh))

    def level_sums():
        lanes = lax.broadcasted_iota(jnp.int32, (n, w), 1)
        acc = jnp.zeros((n, w), F32)
        for l in range(LV_ALL):
            acc = jnp.where(lanes == l, jnp.sum(lev[l], axis=1, keepdims=True), acc)
        hb[hd] = acc.T[:8, :]
        for d in range(1, nh):
            h_send(d).start()

    def x_blocks():
        def fx_all(l):
            fwd(l, x).start()
            for d in (1, 3, 2):
                fx_in(l, d).wait_recv()
                fwd(l, (x + NX - d) % NX).start()

        @pl.when(x % 2 == 1)
        def _():
            fx_all(1)

        @pl.when(x >= 2)
        def _():
            fx_all(2)

    def from_partner(levels_in):
        for l in levels_in:
            @pl.when(bits[l] == 1)
            def _():
                loop(half, lambda i: fwd_in(l, i).wait_recv())

    def plane_gradient():
        @pl.when(z % 2 == 0)
        def _():
            for d in (0, 1, 3, 2):
                bs_in(0, d).wait_recv()
            dp[...] = rsg[0, 0] + rsg[0, 1] + rsg[0, 2] + rsg[0, 3]

            @pl.when(z != 6)
            def _():
                b4_send().wait_recv()
                dp[...] += rz4[...]

        for c in range(4):
            frm, l = b_plan[c]

            @pl.when(x != frm)
            def _():
                bx_in(c, l).wait_recv()

        t = dp[...]
        both = rsx[2] + rsx[3]
        lo[0] = pf(0, r0) * t + rsx[0] + bf(1, r0) * both
        lo[1] = pf(1, r0) * t + both
        lo[2] = pf(2, r0) * t + rsx[1]
        lo[3] = pf(3, r0) * t
        db[x] = lo[x]
        for d in (2, 1, 3):
            d_send(d).start()

    def finish_sources():
        for d in (1, 3, 2):
            d_in(d).wait_recv()

        loop(half, b1)
        loop(half, lambda i: b1_up_in(i).wait_recv())
        loop(heads, sources)

    def blocks_45():
        @pl.when(bits[3] == 1)
        def _():
            hand_on(0)

        @pl.when(bits[4] == 1)
        def _():
            hand_on(1)

    def chain_down():
        for j in range(2):
            b5_in(j).wait_recv()
        t = rz5[0] + rz5[1]
        za[0] = bf(3, r0) * t
        b4_send().start()
        dp[...] = t


    def drain():
        for j in range(7):
            g1(j).wait_send()
        for d in range(1, NZ):
            g3(d).wait_send()
        loop(half, lambda i: f1_send(other(i)).wait_send())

        @pl.when(core == 0)
        def _():
            loop(half, lambda i: f1_send(own(i)).wait_send())

        @pl.when(core == 1)
        def _():
            loop(half, lambda i: b1_early(i).wait_send())

        for d in range(1, NX):
            rs_send(d).wait_send()

        for c in range(4):
            @pl.when(x != x_plan[c][0])
            def _():
                fx_send(c).wait_send()

            frm, l = b_plan[c]

            @pl.when(x == frm)
            def _():
                for d in range(1, NX):
                    bx_send(c, l, d).wait_send()

        for l in range(1, LV):
            @pl.when(bits[l] == 1)
            def _():
                loop(half, lambda i: fwd(l, i).wait_send())
                loop(half, lambda i: gp_send(l, i).wait_send())

        for m in range(3):
            @pl.when(bits[3 + m] == 1)
            def _():
                for d in range(1 if m else 0, NX):
                    bs_send(m, d).wait_send()
                if m:
                    for d in range(1, NX):
                        ag_send(m, d).wait_send()

        @pl.when(z % 2 == 0)
        def _():
            z4_send().wait_send()
            for d in range(1, NX):
                z4_round(d).wait_send()

        @pl.when(z % 4 == 1)
        def _():
            z5_send(1).wait_send()
            z5_send(2).wait_send()

        @pl.when(z == 3)
        def _():
            for d in range(1, 5):
                z6_send(d).wait_send()

        @pl.when(z >= 4)
        def _():
            b6_send().wait_send()

        @pl.when(bits[4] == 1)
        def _():
            b5_send().wait_send()

        @pl.when((z % 2 == 1) & (z != 7))
        def _():
            b4_send().wait_send()

    @pl.when(z == 7)
    def _():
        dp[...] = jnp.zeros((w, w), F32)

    loop(2, lambda i: inside(4 + i))
    @pl.when(bits[4] == 1)
    def _():
        bs_sum(1)

        @pl.when(z != 3)
        def _():
            za[1] = gp[1]
            b5_send().start()

    @pl.when(core == 1)
    def _():
        loop(half, lambda i: f1_send(2 * i).wait_recv())

    @pl.when(z < 4)
    def _():
        @pl.when(z == 3)
        def _():
            for j in range(4):
                b6_in(j).wait_recv()
            t = rz6[0] + rz6[1] + rz6[2] + rz6[3]
            za[1] = gp[1] + bf(4, r0) * t
            b5_send().start()
            za[0] = bf(3, r0) * t
            b4_send().start()
            dp[...] = t

        loop(2, lambda i: inside(6 + i))

        @pl.when(z == 1)
        def _():
            chain_down()

        @pl.when(z != 0)
        def _():
            plane_gradient()

        blocks_45()
        x_blocks()
        from_partner(range(1, 5))
        levels((0, 2))
        levels((4,))
        level_sums()
        drain()

        @pl.when(z == 0)
        def _():
            plane_gradient()

        finish_sources()

    @pl.when(z >= 4)
    def _():
        @pl.when(z == 5)
        def _():
            chain_down()

        z6_send(1).wait_recv()
        hand_round(2)
        loop(2, lambda i: inside(6 + i))
        plane_gradient()
        x_blocks()
        blocks_45()
        from_partner(range(1, 5))
        levels((0, 2))
        hand_on(2)
        from_partner((5,))
        levels((4,))
        level_sums()
        finish_sources()
        drain()

    for d in range(1, nh):
        h_send(d).wait_recv()
    tot = hb[0] + hb[1] + hb[2] + hb[3]
    glt[...] = tot[:LV_ALL, :]

    for d in range(1, nh):
        h_send(d).wait_send()
    for d in range(1, NX):
        d_send(d).wait_send()
    loop(half, lambda i: b1_up(i).wait_send())


def on_device(queries, key_input, value_input, grad_output, log_decay, level_weight, segment):
    n, heads = log_decay.shape
    width = queries.shape[1]
    w = 128
    half = heads // 2
    dma = pltpu.SemaphoreType.DMA

    def mem(*shape):
        return pltpu.VMEM(shape, F32)

    scratch = [mem(n, width) for _ in range(4)] + [mem(w, n)]
    scratch += [mem(heads, n, w), mem(heads, n, w), mem(heads, n, w), mem(LV_ALL, n, w),
                mem(w, n), mem(n, n), mem(LV, 8, w), mem(LV, 8, w), mem(LV, 8, w), mem(NX, 8, w), mem(LV_ALL, n, w)]
    scratch += [mem(8, 8, w), mem(NZ, 8, w), mem(heads, w, w), mem(LV, heads, w, w),
                mem(half, w, w), mem(w, w), mem(NX, w, w), mem(3, w, w),
                mem(LV, heads, w, w), mem(LV - 1, half, w, w), mem(3, half, w, w), mem(3, NX, w, w),
                mem(3, w, w), mem(2, w, w), mem(4, w, w), mem(2, w, w), mem(w, w), mem(NX, w, w)]
    scratch += [mem(2, half, w, w), mem(4, w, w), mem(NX, w, w), mem(w, w), mem(half, w, w)] + [mem(heads, w, w), mem(half, w, w), mem(4, 8, n),
                pltpu.VMEM((heads, w, 3 * n), BF16)]
    scratch += [dma((4,))]
    for a, b in (((14,), (14,)), ((heads,), (heads,)), ((3,), (3,)), ((4,), (2, 3)), ((7,), (3,)),
                 ((3, 3), (3, 3)), ((LV - 1, half), (LV - 1, half)), ((LV - 1, half), (LV - 1, half)),
                 ((3, 4), (3, 4)), ((3,), (7,)), ((3,), (3,)), ((2, 3), (4,)),
                 ((heads,), (heads,)), ((3,), (3,))):
        scratch += [dma(a), dma(b)]
    vm = pl.BlockSpec(memory_space=pltpu.VMEM)
    hbm = pl.BlockSpec(memory_space=pl.ANY)
    out = pltpu.VMEM((n, width), F32)
    dq, dk, dv, glt = pl.pallas_call(
        kernel,
        out_shape=(out, out, out, pltpu.VMEM((LV_ALL, n), F32)),
        in_specs=[vm] * 3 + [hbm] * 4,
        out_specs=(vm,) * 4,
        scratch_shapes=scratch,
        compiler_params=pltpu.CompilerParams(
            collective_id=0, has_side_effects=True, vmem_limit_bytes=60 << 20),
    )(log_decay.T, level_weight.T, segment[None, :], queries, key_input, value_input, grad_output)
    return dq, dk, dv, glt.T


def solution(mesh):
    in_specs = (
        P("seq", "head"),
        P("seq", "head"),
        P("seq", "head"),
        P("seq", "head"),
        P("seq", "head"),
        P("seq", None),
        P("seq"),
    )
    out_specs = (P("seq", "head"), P("seq", "head"), P("seq", "head"), P("seq", None))
    return jax.shard_map(
        on_device, mesh=mesh, in_specs=in_specs, out_specs=out_specs, check_vma=False
    )
```

```python
import jax
import jax.numpy as jnp
from jax import lax
from jax.experimental import pallas as pl
from jax.experimental.pallas import tpu as pltpu
from jax.sharding import PartitionSpec as P

F32 = jnp.float32
BF16 = jnp.bfloat16
NZ, NX = 8, 4
LV_ALL = 7
LV = 6


def split(a):
    hi = a.astype(BF16)
    return hi, (a - hi.astype(F32)).astype(BF16)


def left(a, axis):
    hi, lo = split(a)
    return jnp.concatenate([hi, hi, lo], axis=axis)


def right(a, axis):
    hi, lo = split(a)
    return jnp.concatenate([hi, lo, hi], axis=axis)


def mm(a, b, ca, cb):
    return lax.dot_general(a, b, (((ca,), (cb,)), ((), ())), preferred_element_type=F32)


def loop(n, fn):
    def body(i, carry):
        fn(i)
        return carry

    lax.fori_loop(0, n, body, 0)


def kernel(ldt, lwt, sgt, q_hbm, k_hbm, v_hbm, o_hbm, dq, dk, dv, glt,
           q, k, v, o, packt,
           cumcol, ecol, swcol, lwcol, cumt, bias, bfac, gfac, hfac, pfac, lev,
           pb, zt, st, rf, tt, t01, rsb, zs, gs, gr, gx, rsg, gp, za, rz6, rz5, rz4, db,
           gxx, rsx, lo, dp, ge, rl, ml, hb, olhs,
           s_in, s_g, r_g, s_1, r_1, s_rs, r_rs, s_x, r_x, s_z, r_z, s_ag, r_ag, s_f, r_f, s_p, r_p,
           s_bs, r_bs, s_bz, r_bz, s_d, r_d, s_m, r_m, s_b1, r_b1, s_h, r_h):
    n, heads, w = q.shape[0], swcol.shape[0], 128
    half = heads // 2
    me = lax.axis_index("seq")
    hd = lax.axis_index("head")
    nh = 4
    core = me % 2
    x = (me // 2) % NX
    z = me // (2 * NX)
    bits = [core, x % 2, x // 2, z % 2, (z // 2) % 2, z // 4]
    r0 = x * 2 + core

    def at(zz, xx, cc):
        return ((zz * NX + xx) * 2 + cc, hd)

    partner = at(z, x, 1 - core)

    def cp(src, dst, ss, rs, dev):
        return pltpu.make_async_remote_copy(
            src_ref=src, dst_ref=dst, send_sem=ss, recv_sem=rs,
            device_id=dev, device_id_type=pl.DeviceIdType.MESH)

    def bring(j):
        src, dst = ((k_hbm, k), (v_hbm, v), (o_hbm, o), (q_hbm, q))[j]
        return pltpu.make_async_copy(src, dst, s_in.at[j])

    for j in range(4):
        bring(j).start()

    barrier = pltpu.get_barrier_semaphore()
    plane_peers = [(d, e) for d in range(NX) for e in range(2) if (d, e) != (0, 0)]

    def plane_dev(d, e):
        return at(z, (x + d) % NX, (core + e) % 2)

    peers = [plane_dev(d, e) for d, e in plane_peers]
    peers += [at((z + d) % NZ, x, core) for d in range(1, NZ)]
    peers += [at((z + e) % NZ, (x + d) % NX, core) for d in range(1, NX) for e in (1, NZ - 1)]
    peers += [(me, (hd + d) % nh) for d in range(1, nh)]
    for dev in peers:
        pl.semaphore_signal(barrier, inc=1, device_id=dev, device_id_type=pl.DeviceIdType.MESH)

    packt[...] = jnp.zeros((w, n), F32)
    packt[0:heads, :] = ldt[...]
    packt[8:8 + LV_ALL, :] = lwt[...]
    packt[15:16, :] = sgt[...].astype(F32)
    pk = packt[...].T
    rows = lax.broadcasted_iota(jnp.int32, (n, n), 0)
    cols = lax.broadcasted_iota(jnp.int32, (n, n), 1)
    tri = (cols <= rows).astype(BF16)
    p1 = pk.astype(BF16)
    rest = pk - p1.astype(F32)
    p2 = rest.astype(BF16)
    p3 = (rest - p2.astype(F32)).astype(BF16)
    cum = mm(tri, p1, 1, 0) + mm(tri, p2, 1, 0) + mm(tri, p3, 1, 0)
    total = cum[n - 1:n, :]
    seg = pk[:, 15:16]
    own_end = pk[n - 1:n, 15:16]
    lane1 = lax.broadcasted_iota(jnp.int32, (1, w), 1)
    own_row = jnp.where(lane1 == heads, jnp.broadcast_to(own_end, (1, w)), total)
    own_row = jnp.where(lane1 == heads + 1, jnp.broadcast_to(pk[0:1, 15:16], (1, w)), own_row)
    pb[r0] = jnp.broadcast_to(own_row, (8, w))

    sw = jnp.exp(total - cum) * (seg == own_end).astype(F32)
    for h in range(heads):
        swcol[h] = jnp.broadcast_to(sw[:, h:h + 1], (n, w))

    def own(i):
        return 2 * i + core

    def other(i):
        return 2 * i + 1 - core

    def f1_send(h):
        return cp(st.at[h], rf.at[0, h], s_1.at[h], r_1.at[h], partner)

    def head_cols(h):
        return pl.ds(pl.multiple_of(h * w, w), w)

    bring(0).wait()
    bring(1).wait()

    def make_state(h):
        vt = v[:, head_cols(h)].T
        st[h] = mm(left(vt, 1), right(k[:, head_cols(h)] * swcol[h], 0), 1, 0)

    def state_other(i):
        make_state(other(i))

    def state_own(i):
        make_state(own(i))

        @pl.when(core == 0)
        def _():
            f1_send(own(i)).start()

    first = pk[0:1, 15:16]
    ecum = jnp.exp(cum) * (seg == first).astype(F32)
    for h in range(heads):
        ecol[h] = jnp.broadcast_to(ecum[:, h:h + 1], (n, w))
    for l in range(LV_ALL):
        lwcol[l] = jnp.broadcast_to(pk[:, 8 + l:9 + l], (n, w))


    @pl.when(z < 4)
    def _():
        loop(half, state_other)

    pl.semaphore_wait(barrier, len(peers))
    def g1(j):
        d, e = plane_peers[j]
        return cp(pb.at[r0], pb.at[r0], s_g.at[j], r_g.at[j], plane_dev(d, e))

    def g3(d):
        return cp(zt.at[z], zt.at[z], s_g.at[6 + d], r_g.at[6 + d], at((z + d) % NZ, x, core))

    for j in range(7):
        g1(j).start()

    @pl.when(z >= 4)
    def _():
        loop(half, state_other)

    loop(half, lambda i: f1_send(other(i)).start())
    loop(half, state_own)
    def gp_send(l, i):
        return cp(gs.at[l, other(i)], gr.at[l - 1, i], s_p.at[l - 1, i], r_p.at[l - 1, i], partner)

    def make_g(h, l):
        if l == 4:
            olhs[h] = left(o[:, head_cols(h)].T, 1)
        lhs = olhs[h]
        qe = q[:, head_cols(h)] * ecol[h]
        a = jnp.concatenate([qe * lwcol[l + 1], qe * lwcol[l + 2]], axis=1)
        both = mm(lhs, right(a, 0), 1, 0)
        gs[l, h] = both[:, :w]
        gs[l + 1, h] = both[:, w:]

    def g_other(l):
        def one(i):
            make_g(other(i), l)
            for m in (l + 1, l):
                if m:
                    @pl.when(bits[m] == 1)
                    def _():
                        gp_send(m, i).start()

        return one

    def g_own(l):
        def one(i):
            make_g(own(i), l)

        return one

    bring(2).wait()
    bring(3).wait()
    loop(half, g_other(4))
    loop(half, g_own(4))
    for j in range(7):
        g1(j).wait_recv()
    sub = lax.broadcasted_iota(jnp.int32, (8, w), 0)
    lane8 = lax.broadcasted_iota(jnp.int32, (8, w), 1)
    plane = jnp.zeros((8, w), F32)
    for r in range(8):
        plane = jnp.where(sub == r, pb[r], plane)
    zt[z] = plane
    for d in range(1, NZ):
        g3(d).start()

    def tools(tbl, idx):
        def row(c):
            return jnp.sum(jnp.where(idx == c, tbl, 0.0), axis=0, keepdims=True)

        def span(lo, hi):
            inside_span = jnp.where((idx > lo) & (idx <= hi), tbl, 0.0)
            return jnp.exp(jnp.minimum(jnp.sum(inside_span, axis=0, keepdims=True), 0.0))

        def same(a, b):
            return (row(a)[:, heads:heads + 1] == row(b)[:, heads:heads + 1]).astype(F32)

        return row, span, same

    def spread(vec):
        m = jnp.where(lane8 == sub, jnp.broadcast_to(vec, (8, w)), 0.0)
        return jnp.broadcast_to(jnp.sum(m, axis=1, keepdims=True), (8, w))

    row, span, same = tools(plane, sub)
    for l, low in ((0, 2 * x), (1, 1)):
        up = low + (1 << l)
        bfac[l] = spread(span(low, up) * same(low, up))
    for j in range(NX):
        pfac[j] = spread(span(2 * j + 1, 7) * same(2 * j + 1, 7))

    def bf(l, h):
        return bfac[l, pl.ds(h, 1), :]

    def gf(l, h):
        return gfac[l, pl.ds(h, 1), :]

    def pf(j, h):
        return pfac[j, pl.ds(h, 1), :]

    def rs_send(d):
        i = (x + d) % NX
        return cp(tt.at[i], rsb.at[x], s_rs.at[d - 1], r_rs.at[d - 1], at(z, i, core))

    def rs_in(d):
        j = (x + NX - d) % NX
        return cp(tt.at[x], rsb.at[j], s_rs.at[d - 1], r_rs.at[d - 1], at(z, j, core))

    def f1(i):
        h = own(i)
        f1_send(h).wait_recv()
        b = bf(0, h)
        u = core == 1
        tt[i] = jnp.where(u, 1.0, b) * st[h] + jnp.where(u, b, 1.0) * rf[0, h]

    loop(half, f1)
    for d in (2, 1, 3):
        rs_send(d).start()

    loop(half, g_other(2))
    for h in range(heads):
        cumcol[h] = jnp.broadcast_to(cum[:, h:h + 1], (n, w))
    cumt[...] = cum.T
    segrow = packt[15:16, :]
    vis = (cols <= rows) & (jnp.broadcast_to(seg, (n, n)) == jnp.broadcast_to(segrow, (n, n)))
    bias[...] = jnp.where(vis, 0.0, -1e30)
    for l in range(LV_ALL):
        lev[l] = jnp.zeros((n, w), F32)

    loop(half, g_own(2))
    loop(half, g_other(0))
    loop(half, g_own(0))

    for d in (1, 3, 2):
        rs_in(d).wait_recv()
    rsb[x] = tt[x]
    acc = pf(0, r0) * rsb[0]
    for j in range(1, NX):
        acc = acc + pf(j, r0) * rsb[j]
    zs[0] = acc

    def z4_send():
        return cp(zs.at[0], rf.at[3, r0], s_z.at[0], r_z.at[0], at((z + 1) % NZ, x, core))

    def z5_send(d):
        return cp(zs.at[1], rf.at[4, r0], s_z.at[d], r_z.at[1], at((z + d) % NZ, x, core))

    def z6_send(d):
        return cp(zs.at[2], rf.at[5, r0], s_z.at[2 + d], r_z.at[2], at((z + d) % NZ, x, core))

    def z4_round(d):
        return cp(zs.at[0], rf.at[3, r0], s_ag.at[0, d - 1], r_ag.at[0, d - 1], at((z + 1) % NZ, (x + d) % NX, core))

    @pl.when(z % 2 == 0)
    def _():
        z4_send().start()
        for d in (2, 1, 3):
            z4_round(d).start()

    for d in range(1, NZ):
        g3(d).wait_recv()
    row, span, same = tools(zt[...].reshape(8 * NZ, w), lax.broadcasted_iota(jnp.int32, (8 * NZ, w), 0))
    def starts(r):
        c = z * 2 * NX + r
        return (row(c)[:, heads + 1:heads + 2] == row(c - 1)[:, heads:heads + 1]).astype(F32)

    for l in range(LV):
        hs = 1 << l
        low = (me // (2 * hs)) * (2 * hs) + hs - 1
        prev = me - 1
        gfac[l] = spread(span(low, prev) * same(low, prev) * starts(r0) * bits[l].astype(F32))
        if l:
            other_prev = me - 2 * core
            hfac[l] = spread(span(low, other_prev) * same(low, other_prev) * starts(r0 + 1 - 2 * core) * bits[l].astype(F32))
        if l in (3, 4):
            bfac[l] = spread(span(low, low + hs) * same(low, low + hs))
    def gsum(l, i):
        return gs[l, own(i)] * gf(l, own(i)) + gr[l - 1, i] * hfac[l, pl.ds(own(i), 1), :]

    def bs_send(m, d):
        i = (x + d) % NX
        to = z if m else (z + NZ - 1) % NZ
        return cp(gx.at[m, i], rsg.at[m, x], s_bs.at[m, (d + 3) % 4], r_bs.at[m, (d + 3) % 4], at(to, i, core))

    def bs_in(m, d):
        j = (x + NX - d) % NX
        frm = z if m else (z + 1) % NZ
        return cp(gx.at[m, x], rsg.at[m, j], s_bs.at[m, (d + 3) % 4], r_bs.at[m, (d + 3) % 4], at(frm, j, core))

    def bs_out(m):
        @pl.when(bits[3 + m] == 1)
        def _():
            def one(i):
                gp_send(3 + m, i).wait_recv()
                gx[m, i] = gsum(3 + m, i)

            loop(half, one)
            for d in (2, 1, 3) if m else (2, 1, 3, 0):
                bs_send(m, d).start()

    def bs_sum(m):
        for d in (1, 3, 2):
            bs_in(m, d).wait_recv()
        t = gx[m, x]
        for d in range(1, NX):
            t = t + rsg[m, (x + NX - d) % NX]
        gp[m] = t

    def inside(h):
        hc = head_cols(h)
        qh, kh, vh, oh = q[:, hc], k[:, hc], v[:, hc], o[:, hc]
        cc = cumcol[h]
        gap = jnp.concatenate([cc, cc], axis=1) - cumt[pl.ds(h, 1), :]
        within = jnp.exp(jnp.minimum(gap, 0.0) + bias[...])
        sc = mm(left(qh, 1), right(kh, 1), 1, 1)
        go = mm(left(oh, 1), right(vh, 1), 1, 1)
        lw = lwcol[0]
        wt = within * jnp.concatenate([lw, lw], axis=1)
        prod = within * sc * go
        lev[0] += prod[:, :w] + prod[:, w:]
        a = wt * sc
        b = wt * go
        dq[:, hc] = mm(left(b, 1), right(kh, 0), 1, 0)
        dv[:, hc] = mm(left(a.T, 1), right(oh, 0), 1, 0)
        dk[:, hc] = mm(left(b.T, 1), right(qh, 0), 1, 0)

    bs_out(2)
    bs_out(1)
    bs_out(0)
    loop(2, inside)

    def ag_send(m, d):
        slot = rf.at[3 + m, r0]
        return cp(slot, slot, s_ag.at[m, d - 1], r_ag.at[m, d - 1], at(z, (x + d) % NX, core))

    def ag_in(m, d):
        slot = rf.at[3 + m, own((x + NX - d) % NX)]
        return cp(slot, slot, s_ag.at[m, d - 1], r_ag.at[m, d - 1], at(z, (x + NX - d) % NX, core))

    def fwd(l, i):
        slot = rf.at[l, own(i)]
        return cp(slot, slot, s_f.at[l - 1, i], r_f.at[l - 1, i], partner)

    def fwd_in(l, i):
        slot = rf.at[l, other(i)]
        return cp(slot, slot, s_f.at[l - 1, i], r_f.at[l - 1, i], partner)

    def hand_round(m):
        for d in (2, 1, 3):
            ag_send(m, d).start()
        fwd(3 + m, x).start()

    def hand_on(m):
        for d in (1, 3, 2):
            ag_in(m, d).wait_recv()
            fwd(3 + m, (x + NX - d) % NX).start()

    @pl.when(z % 2 == 1)
    def _():
        z4_send().wait_recv()
        zs[1] = bf(3, r0) * rf[3, r0] + zs[0]

        @pl.when((z // 2) % 2 == 0)
        def _():
            z5_send(2).start()
            z5_send(1).start()

    @pl.when(z % 2 == 1)
    def _():
        fwd(3, x).start()

    def bx_send(c, l, d):
        i = (x + d) % NX
        return cp(gxx.at[l - 1, i], rsx.at[c], s_m.at[l - 1, d - 1], r_m.at[c], at(z, i, core))

    def bx_in(c, l):
        return cp(gxx.at[l - 1, x], rsx.at[c], s_m.at[l - 1, 0], r_m.at[c], at(z, x, 1 - core))

    b_plan = ((1, 1), (3, 1), (2, 2), (3, 2))
    for c in (2, 3, 0, 1):
        frm, l = b_plan[c]

        @pl.when(x == frm)
        def _():
            def one(i):
                gp_send(l, i).wait_recv()
                gxx[l - 1, i] = gsum(l, i)

            loop(half, one)
            rsx[c] = gxx[l - 1, x]
            for d in (2, 1, 3):
                bx_send(c, l, d).start()

    t01[...] = bf(1, r0) * rsb[0] + rsb[1]
    x_plan = ((1, 1, 0), (3, 1, 2), (2, 2, None), (3, 2, None))

    def fx_send(c):
        to, l, j = x_plan[c]
        src = t01 if j is None else rsb.at[j]
        return cp(src, rf.at[l, r0], s_x.at[c], r_x.at[l - 1, (to + NX - x + 3) % NX], at(z, to, core))

    def fx_in(l, d):
        j = (x + NX - d) % NX
        return cp(t01, rf.at[l, own(j)], s_x.at[0], r_x.at[l - 1, d - 1], at(z, j, core))

    for c in range(4):
        to, l, j = x_plan[c]

        @pl.when(x == to)
        def _():
            rf[l, r0] = t01[...] if j is None else rsb[j]

        @pl.when(x != to)
        def _():
            fx_send(c).start()

    def b6_send():
        return cp(gp.at[2], rz6.at[z % 4], s_bz.at[0], r_bz.at[z % 4], at(3, x, core))

    def b6_in(j):
        return cp(gp.at[2], rz6.at[j], s_bz.at[0], r_bz.at[j], at(4 + j, x, core))

    def b5_send():
        return cp(za.at[1], rz5.at[z % 2], s_bz.at[1], r_bz.at[4 + z % 2], at(4 * (z // 4) + 1, x, core))

    def b5_in(j):
        return cp(za.at[1], rz5.at[j], s_bz.at[1], r_bz.at[4 + j], at((z + 1 + j) % NZ, x, core))

    def b4_send():
        return cp(za.at[0], rz4, s_bz.at[2], r_bz.at[6], at((z + NZ - 1) % NZ, x, core))

    @pl.when(z >= 4)
    def _():
        bs_sum(2)
        b6_send().start()

    loop(2, lambda i: inside(2 + i))

    @pl.when(z == 3)
    def _():
        z5_send(1).wait_recv()
        zs[2] = bf(4, r0) * rf[4, r0] + zs[1]
        for d in (4, 3, 2, 1):
            z6_send(d).start()

    @pl.when(bits[4] == 1)
    def _():
        @pl.when(z != 3)
        def _():
            z5_send(1).wait_recv()

        hand_round(1)

    def b1_early(i):
        return cp(ge.at[i], rl.at[2 * i], s_b1.at[i], r_b1.at[i], partner)

    @pl.when(core == 1)
    def _():
        def one(i):
            ge[i] = gs[0, 2 * i] * gf(0, 2 * i)
            b1_early(i).start()

        loop(half, one)

    def d_send(d):
        return cp(lo.at[(x + d) % NX], db.at[x], s_d.at[d - 1], r_d.at[d - 1], at(z, (x + d) % NX, core))

    def d_in(d):
        return cp(lo.at[x], db.at[(x + NX - d) % NX], s_d.at[d - 1], r_d.at[d - 1], at(z, (x + NX - d) % NX, core))

    def b1_up(i):
        return cp(ml.at[i], rl.at[own(i)], s_b1.at[half + i], r_b1.at[half + i], partner)

    def b1_up_in(i):
        return cp(ml.at[i], rl.at[other(i)], s_b1.at[half + i], r_b1.at[half + i], partner)

    def b1(i):
        h = own(i)
        lam = db[i]

        @pl.when(core == 1)
        def _():
            ml[i] = bf(0, h) * lam + gs[0, h] * gf(0, h)
            rl[h] = lam

        @pl.when(core == 0)
        def _():
            ml[i] = lam
            b1_early(i).wait_recv()
            rl[h] = bf(0, h) * lam + rl[h]

        b1_up(i).start()

    def levels(pairs):
        def one(h):
            hc = head_cols(h)
            oh = left(o[:, hc], 1)
            qh = q[:, hc]
            e = ecol[h]
            acc = dq[:, hc]
            for l in pairs:
                pair = []
                for m in (l, l + 1):
                    pair.append(jnp.where(bits[m] == 1, rf[m, h] * gf(m, h), 0.0))
                back = mm(oh, right(jnp.concatenate(pair, axis=1), 0), 1, 0)
                for m in (l, l + 1):
                    part = e * back[:, (m - l) * w:(m - l + 1) * w]
                    lev[m + 1] += qh * part
                    acc = acc + lwcol[m + 1] * part
            dq[:, hc] = acc

        loop(heads, one)

    def sources(h):
        hc = head_cols(h)
        g = rl[h]
        s = swcol[h]
        dk[:, hc] += s * mm(left(v[:, hc], 1), right(g, 0), 1, 0)
        dv[:, hc] += s * mm(left(k[:, hc], 1), right(g, 1), 1, 1)

    def h_send(d):
        return cp(hb.at[hd], hb.at[hd], s_h.at[d - 1], r_h.at[d - 1], (me, (hd + d) % nh))

    def level_sums():
        lanes = lax.broadcasted_iota(jnp.int32, (n, w), 1)
        acc = jnp.zeros((n, w), F32)
        for l in range(LV_ALL):
            acc = jnp.where(lanes == l, jnp.sum(lev[l], axis=1, keepdims=True), acc)
        hb[hd] = acc.T[:8, :]
        for d in range(1, nh):
            h_send(d).start()

    def x_blocks():
        def fx_all(l):
            fwd(l, x).start()
            for d in (1, 3, 2):
                fx_in(l, d).wait_recv()
                fwd(l, (x + NX - d) % NX).start()

        @pl.when(x % 2 == 1)
        def _():
            fx_all(1)

        @pl.when(x >= 2)
        def _():
            fx_all(2)

    def from_partner(levels_in):
        for l in levels_in:
            @pl.when(bits[l] == 1)
            def _():
                loop(half, lambda i: fwd_in(l, i).wait_recv())

    def plane_gradient():
        @pl.when(z % 2 == 0)
        def _():
            for d in (0, 1, 3, 2):
                bs_in(0, d).wait_recv()
            dp[...] = rsg[0, 0] + rsg[0, 1] + rsg[0, 2] + rsg[0, 3]

            @pl.when(z != 6)
            def _():
                b4_send().wait_recv()
                dp[...] += rz4[...]

        for c in range(4):
            frm, l = b_plan[c]

            @pl.when(x != frm)
            def _():
                bx_in(c, l).wait_recv()

        t = dp[...]
        both = rsx[2] + rsx[3]
        lo[0] = pf(0, r0) * t + rsx[0] + bf(1, r0) * both
        lo[1] = pf(1, r0) * t + both
        lo[2] = pf(2, r0) * t + rsx[1]
        lo[3] = pf(3, r0) * t
        db[x] = lo[x]
        for d in (2, 1, 3):
            d_send(d).start()

    def finish_sources():
        for d in (1, 3, 2):
            d_in(d).wait_recv()

        loop(half, b1)
        loop(half, lambda i: sources(own(i)))
        loop(half, lambda i: b1_up_in(i).wait_recv())
        loop(half, lambda i: sources(other(i)))

    def blocks_45():
        @pl.when(bits[3] == 1)
        def _():
            hand_on(0)

        @pl.when(bits[4] == 1)
        def _():
            hand_on(1)

    def chain_down():
        for j in range(2):
            b5_in(j).wait_recv()
        t = rz5[0] + rz5[1]
        za[0] = bf(3, r0) * t
        b4_send().start()
        dp[...] = t


    def drain():
        for j in range(7):
            g1(j).wait_send()
        for d in range(1, NZ):
            g3(d).wait_send()
        loop(half, lambda i: f1_send(other(i)).wait_send())

        @pl.when(core == 0)
        def _():
            loop(half, lambda i: f1_send(own(i)).wait_send())

        @pl.when(core == 1)
        def _():
            loop(half, lambda i: b1_early(i).wait_send())

        for d in range(1, NX):
            rs_send(d).wait_send()

        for c in range(4):
            @pl.when(x != x_plan[c][0])
            def _():
                fx_send(c).wait_send()

            frm, l = b_plan[c]

            @pl.when(x == frm)
            def _():
                for d in range(1, NX):
                    bx_send(c, l, d).wait_send()

        for l in range(1, LV):
            @pl.when(bits[l] == 1)
            def _():
                loop(half, lambda i: fwd(l, i).wait_send())
                loop(half, lambda i: gp_send(l, i).wait_send())

        for m in range(3):
            @pl.when(bits[3 + m] == 1)
            def _():
                for d in range(1 if m else 0, NX):
                    bs_send(m, d).wait_send()
                if m:
                    for d in range(1, NX):
                        ag_send(m, d).wait_send()

        @pl.when(z % 2 == 0)
        def _():
            z4_send().wait_send()
            for d in range(1, NX):
                z4_round(d).wait_send()

        @pl.when(z % 4 == 1)
        def _():
            z5_send(1).wait_send()
            z5_send(2).wait_send()

        @pl.when(z == 3)
        def _():
            for d in range(1, 5):
                z6_send(d).wait_send()

        @pl.when(z >= 4)
        def _():
            b6_send().wait_send()

        @pl.when(bits[4] == 1)
        def _():
            b5_send().wait_send()

        @pl.when((z % 2 == 1) & (z != 7))
        def _():
            b4_send().wait_send()

    @pl.when(z == 7)
    def _():
        dp[...] = jnp.zeros((w, w), F32)

    loop(2, lambda i: inside(4 + i))
    @pl.when(bits[4] == 1)
    def _():
        bs_sum(1)

        @pl.when(z != 3)
        def _():
            za[1] = gp[1]
            b5_send().start()

    @pl.when(core == 1)
    def _():
        loop(half, lambda i: f1_send(2 * i).wait_recv())

    @pl.when(z < 4)
    def _():
        @pl.when(z == 3)
        def _():
            for j in range(4):
                b6_in(j).wait_recv()
            t = rz6[0] + rz6[1] + rz6[2] + rz6[3]
            za[1] = gp[1] + bf(4, r0) * t
            b5_send().start()
            za[0] = bf(3, r0) * t
            b4_send().start()
            dp[...] = t

        loop(2, lambda i: inside(6 + i))

        @pl.when(z == 1)
        def _():
            chain_down()

        @pl.when(z != 0)
        def _():
            plane_gradient()

        blocks_45()
        x_blocks()
        from_partner(range(1, 5))
        levels((0, 2))
        levels((4,))
        level_sums()
        drain()

        @pl.when(z == 0)
        def _():
            plane_gradient()

        finish_sources()

    @pl.when(z >= 4)
    def _():
        @pl.when(z == 5)
        def _():
            chain_down()

        z6_send(1).wait_recv()
        hand_round(2)
        loop(2, lambda i: inside(6 + i))
        plane_gradient()
        x_blocks()
        blocks_45()
        from_partner(range(1, 5))
        hand_on(2)
        levels((0, 2))
        from_partner((5,))
        levels((4,))
        level_sums()
        finish_sources()
        drain()

    for d in range(1, nh):
        h_send(d).wait_recv()
    tot = hb[0] + hb[1] + hb[2] + hb[3]
    glt[...] = tot[:LV_ALL, :]

    for d in range(1, nh):
        h_send(d).wait_send()
    for d in range(1, NX):
        d_send(d).wait_send()
    loop(half, lambda i: b1_up(i).wait_send())


def on_device(queries, key_input, value_input, grad_output, log_decay, level_weight, segment):
    n, heads = log_decay.shape
    width = queries.shape[1]
    w = 128
    half = heads // 2
    dma = pltpu.SemaphoreType.DMA

    def mem(*shape):
        return pltpu.VMEM(shape, F32)

    scratch = [mem(n, width) for _ in range(4)] + [mem(w, n)]
    scratch += [mem(heads, n, w), mem(heads, n, w), mem(heads, n, w), mem(LV_ALL, n, w),
                mem(w, n), mem(n, n), mem(LV, 8, w), mem(LV, 8, w), mem(LV, 8, w), mem(NX, 8, w), mem(LV_ALL, n, w)]
    scratch += [mem(8, 8, w), mem(NZ, 8, w), mem(heads, w, w), mem(LV, heads, w, w),
                mem(half, w, w), mem(w, w), mem(NX, w, w), mem(3, w, w),
                mem(LV, heads, w, w), mem(LV - 1, half, w, w), mem(3, half, w, w), mem(3, NX, w, w),
                mem(3, w, w), mem(2, w, w), mem(4, w, w), mem(2, w, w), mem(w, w), mem(NX, w, w)]
    scratch += [mem(2, half, w, w), mem(4, w, w), mem(NX, w, w), mem(w, w), mem(half, w, w)] + [mem(heads, w, w), mem(half, w, w), mem(4, 8, n),
                pltpu.VMEM((heads, w, 3 * n), BF16)]
    scratch += [dma((4,))]
    for a, b in (((14,), (14,)), ((heads,), (heads,)), ((3,), (3,)), ((4,), (2, 3)), ((7,), (3,)),
                 ((3, 3), (3, 3)), ((LV - 1, half), (LV - 1, half)), ((LV - 1, half), (LV - 1, half)),
                 ((3, 4), (3, 4)), ((3,), (7,)), ((3,), (3,)), ((2, 3), (4,)),
                 ((heads,), (heads,)), ((3,), (3,))):
        scratch += [dma(a), dma(b)]
    vm = pl.BlockSpec(memory_space=pltpu.VMEM)
    hbm = pl.BlockSpec(memory_space=pl.ANY)
    out = pltpu.VMEM((n, width), F32)
    dq, dk, dv, glt = pl.pallas_call(
        kernel,
        out_shape=(out, out, out, pltpu.VMEM((LV_ALL, n), F32)),
        in_specs=[vm] * 3 + [hbm] * 4,
        out_specs=(vm,) * 4,
        scratch_shapes=scratch,
        compiler_params=pltpu.CompilerParams(
            collective_id=0, has_side_effects=True, vmem_limit_bytes=60 << 20),
    )(log_decay.T, level_weight.T, segment[None, :], queries, key_input, value_input, grad_output)
    return dq, dk, dv, glt.T


def solution(mesh):
    in_specs = (
        P("seq", "head"),
        P("seq", "head"),
        P("seq", "head"),
        P("seq", "head"),
        P("seq", "head"),
        P("seq", None),
        P("seq"),
    )
    out_specs = (P("seq", "head"), P("seq", "head"), P("seq", "head"), P("seq", None))
    return jax.shard_map(
        on_device, mesh=mesh, in_specs=in_specs, out_specs=out_specs, check_vma=False
    )
```
